512 devices in a mesh: lon: 32 (over x, y_hi, core), head: 16 (over z, y_lo).
Axes of the slice: x: 4, y: 8 (y_hi: 4, y_lo: 2; y = y_hi * 2 + y_lo), z: 8, core: 2. Of those that a mesh axis runs over, the one named last changes fastest.
Arguments:
- latents: bfloat16 [3, 48, 256, 1024], P(None, 'head', 'lon'), may hold values from -16 to 16
- out_grad: bfloat16 [3, 48, 256, 1024], P(None, 'head', 'lon'), may hold values from -6 to 6
- qkv_weight: bfloat16 [16, 1024, 192], P('head'), as said below
- out_weight: bfloat16 [16, 64, 1024], replicated, may hold values from -0.1875 to 0.1875
Outputs:
- mixed: bfloat16 [3, 48, 256, 1024], P(None, 'head', 'lon')
- latent_grad: bfloat16 [3, 48, 256, 1024], P(None, 'head', 'lon')
- qkv_grad: float32 [16, 1024, 192], P('head')
The draws below stay inside these ranges and needn't reach their ends.
Inputs may be any that keep to these rules, and one draw needn't show every extreme that they name: `qkv_weight`: entries lie within -14 / sqrt(1024) and 14 / sqrt(1024).
All inputs are finite; a program needn't handle non-finite values.
Results may differ from the reference program's by a relative error of at most 0.024.
The reference program's roundings to bfloat16 on the way count: a program that leaves them out, or rounds other values in their place, can miss the bound.
Values may be sent and summed in bfloat16 or wider, within the bound.
No kernel may reach another device: no remote copies, remote signals or barrier semaphores. Data moves between devices by JAX's collectives and lax.ppermute only.
A program may use at most 64 MiB of HBM per device.

```python
import jax
import jax.numpy as jnp
from jax import lax

D = 1024
HEADS = 16
HD = 64
LEV = 3
WIN_LAT = 6
WIN_LON = 8
LAT = 48
LON = 256


def draw_latents(key, part):
    key_base = jax.random.fold_in(key, 0)
    full_shape = (LEV, LAT, LON, D)
    normal_draw = jnp.clip(jax.random.normal(key_base, full_shape, jnp.float32), -5.0, 5.0)
    drawn = normal_draw
    return drawn.astype(jnp.bfloat16)


def draw_qkv_weight(key, part):
    key_query, key_keys, key_value = jax.random.split(key, 3)
    factor = D ** (-0.5)
    block_shape = (HEADS, D, HD)
    query_part = jnp.clip(jax.random.normal(key_query, block_shape, jnp.float32), -4.0, 4.0) * factor
    fresh_part = jnp.clip(jax.random.normal(key_keys, block_shape, jnp.float32), -4.0, 4.0) * factor
    value_portion = jnp.clip(jax.random.normal(key_value, block_shape, jnp.float32), -4.0, 4.0) * factor
    key_portion = fresh_part
    return jnp.concatenate([query_part, key_portion, value_portion], axis=-1).astype(jnp.bfloat16)


def block_levels(rng, shape, cuts, least, top_value):
    def one(axis_at, parts):
        draws = jax.random.uniform(jax.random.fold_in(jax.random.fold_in(rng, 6), axis_at), (parts,), jnp.float32, least / len(cuts), top_value / len(cuts))
        return jnp.repeat(jnp.exp(draws), shape[axis_at] // parts).reshape((-1,) + (1,) * (len(shape) - axis_at - 1))

    gain = one(*cuts[0])
    for cut in cuts[1:]:
        gain = gain * one(*cut)
    return gain


def normal_values(stream_key, dims, scale, bound, pieces=(), dtype=jnp.bfloat16):
    level = block_levels(stream_key, dims, pieces, -0.22, 0.18) if pieces else 1.0
    result = jax.random.normal(stream_key, dims, jnp.float32) * scale * level
    return jnp.minimum(jnp.maximum(result, -bound), bound).astype(dtype)


def setup_inputs(seed: int = 0) -> dict:
    seeds = jax.random.split(jax.random.key(seed), 5)
    latents = draw_latents(jax.random.fold_in(seeds[4], 71), 0)
    out_grad = normal_values(seeds[1], (LEV, LAT, LON, D), 1.0, 6.0, ((1, 16), (2, 32)))
    qkv_weight = draw_qkv_weight(jax.random.fold_in(seeds[4], 71), 0)
    out_weight = normal_values(seeds[3], (HEADS, HD, D), (HEADS * HD) ** -0.5, 0.1875)
    return {"latents": latents, "out_grad": out_grad, "qkv_weight": qkv_weight, "out_weight": out_weight}


MASKED = -1e30


def softmax_rows(query_rows, key_rows, valid, score_scale_factor):
    score_matrix = jnp.einsum("fud,fwd->fuw", query_rows.astype(jnp.float32), key_rows.astype(jnp.float32)) * score_scale_factor
    score_matrix = jnp.where(valid[:, None, :], score_matrix, MASKED)
    row_max = jnp.max(score_matrix, axis=-1, keepdims=True)
    powers = jnp.exp(score_matrix - row_max)
    return powers / jnp.sum(powers, axis=-1, keepdims=True)


def head_pass(latents, weight, outer_gradient):
    score_scale_factor = HD ** -0.5
    windows = LAT // WIN_LAT
    blocks = LON // WIN_LON
    key_cols = 2 * WIN_LON
    half_lat = WIN_LAT // 2
    half_lon = WIN_LON // 2
    flat = latents.reshape(-1, D)
    projected = jnp.dot(flat, weight, preferred_element_type=jnp.float32).astype(jnp.bfloat16)
    projected = projected.reshape(LEV, LAT, LON, 3 * HD)
    query_rows = projected[..., :HD].reshape(LEV, windows, WIN_LAT, blocks, WIN_LON, HD)
    query_rows = query_rows.transpose(1, 3, 0, 2, 4, 5).reshape(windows * blocks, LEV * WIN_LAT * WIN_LON, HD)
    col_index = ((WIN_LON * jnp.arange(blocks)[:, None] - WIN_LON // 2 + jnp.arange(key_cols)[None, :]) % LON).astype(jnp.int32)
    kv_cols = projected[..., HD:][:, :, col_index]
    padded = jnp.pad(kv_cols, ((0, 0), (half_lat, half_lat), (0, 0), (0, 0), (0, 0)))
    lower = padded[:, :LAT].reshape(LEV, windows, WIN_LAT, blocks, key_cols, 2 * HD)
    upper = padded[:, WIN_LAT:LAT + WIN_LAT].reshape(LEV, windows, WIN_LAT, blocks, key_cols, 2 * HD)
    joined = jnp.concatenate([lower, upper], axis=2)
    key_value_pairs = joined.transpose(1, 3, 0, 2, 4, 5).reshape(windows * blocks, LEV * 2 * WIN_LAT * key_cols, 2 * HD)
    lat_index = WIN_LAT * jnp.arange(windows)[:, None] - half_lat + jnp.arange(2 * WIN_LAT)[None, :]
    inside = (lat_index >= 0) & (lat_index < LAT)
    valid = jnp.broadcast_to(inside[:, None, None, :, None], (windows, blocks, LEV, 2 * WIN_LAT, key_cols))
    valid = valid.reshape(windows * blocks, -1)
    key_portion = key_value_pairs[..., :HD]
    value_portion = key_value_pairs[..., HD:]
    probs = softmax_rows(query_rows, key_portion, valid, score_scale_factor)
    probabilities_bfloat = probs.astype(jnp.bfloat16)
    attended_values = jnp.einsum("ucf,ufg->ucg", probabilities_bfloat.astype(jnp.float32), value_portion.astype(jnp.float32)).astype(jnp.bfloat16)
    attended_values = attended_values.reshape(windows, blocks, LEV, WIN_LAT, WIN_LON, HD).transpose(2, 0, 3, 1, 4, 5)
    attended_values = attended_values.reshape(LEV, LAT, LON, HD)
    window_gradient = outer_gradient.reshape(LEV, windows, WIN_LAT, blocks, WIN_LON, HD)
    window_gradient = window_gradient.transpose(1, 3, 0, 2, 4, 5).reshape(windows * blocks, LEV * WIN_LAT * WIN_LON, HD)
    probability_gradient = jnp.einsum("fud,fwd->fuw", window_gradient.astype(jnp.float32), value_portion.astype(jnp.float32))
    centre = jnp.sum(probs * probability_gradient, axis=-1, keepdims=True)
    score_gradient = (probs * (probability_gradient - centre)).astype(jnp.bfloat16)
    query_gradient = jnp.einsum("ucf,ufg->ucg", score_gradient.astype(jnp.float32), key_portion.astype(jnp.float32)) * score_scale_factor
    key_gradient = jnp.einsum("txd,txr->tdr", score_gradient.astype(jnp.float32), query_rows.astype(jnp.float32)) * score_scale_factor
    value_gradient = jnp.einsum("txd,txr->tdr", probabilities_bfloat.astype(jnp.float32), window_gradient.astype(jnp.float32))
    query_gradient = query_gradient.reshape(windows, blocks, LEV, WIN_LAT, WIN_LON, HD).transpose(2, 0, 3, 1, 4, 5)
    query_gradient = query_gradient.reshape(LEV, LAT, LON, HD)
    pair_grad = jnp.concatenate([key_gradient, value_gradient], axis=-1)
    pair_grad = pair_grad.reshape(windows, blocks, LEV, 2 * WIN_LAT, key_cols, 2 * HD).transpose(2, 0, 3, 1, 4, 5)
    lower_grad = pair_grad[:, :, :WIN_LAT].reshape(LEV, LAT, blocks, key_cols, 2 * HD)
    upper_grad = pair_grad[:, :, WIN_LAT:].reshape(LEV, LAT, blocks, key_cols, 2 * HD)
    summed = jnp.pad(lower_grad, ((0, 0), (0, WIN_LAT), (0, 0), (0, 0), (0, 0))) + jnp.pad(upper_grad, ((0, 0), (WIN_LAT, 0), (0, 0), (0, 0), (0, 0)))
    trimmed = summed[:, half_lat:half_lat + LAT]
    rounded = lax.optimization_barrier(trimmed.astype(jnp.bfloat16)).astype(jnp.float32)
    col_pos = jnp.arange(key_cols)
    inner = (col_pos >= half_lon) & (col_pos < half_lon + WIN_LON)
    trimmed = jnp.where(inner[None, None, None, :, None], trimmed, rounded)
    kv_grad = jnp.zeros((LEV, LAT, LON, 2 * HD), jnp.float32).at[:, :, col_index].add(trimmed)
    projected_grad = jnp.concatenate([query_gradient, kv_grad], axis=-1).astype(jnp.bfloat16)
    return attended_values, projected_grad


def reference(latents, out_grad, qkv_weight, out_weight):
    flat = latents.reshape(-1, D)
    grad_flat = out_grad.reshape(-1, D)
    out_flat = out_weight.reshape(HEADS * HD, D)
    attended_grad = jnp.dot(grad_flat, out_flat.T, preferred_element_type=jnp.float32).astype(jnp.bfloat16)
    attended_grad = attended_grad.reshape(LEV, LAT, LON, HEADS, HD).transpose(3, 0, 1, 2, 4)

    def per_head(carry, pack):
        mixed_sum, latent_sum = carry
        weight, out_rows, outer_gradient = pack
        attended_values, projected_grad = head_pass(latents, weight, outer_gradient)
        mixed_sum = mixed_sum + jnp.dot(attended_values.reshape(-1, HD), out_rows, preferred_element_type=jnp.float32)
        grad_rows = projected_grad.reshape(-1, 3 * HD)
        latent_sum = latent_sum + jnp.dot(grad_rows, weight.T, preferred_element_type=jnp.float32)
        head_grad = jnp.dot(flat.T, grad_rows, preferred_element_type=jnp.float32)
        return (mixed_sum, latent_sum), head_grad

    start = (jnp.zeros((flat.shape[0], D), jnp.float32), jnp.zeros((flat.shape[0], D), jnp.float32))
    (mixed_sum, latent_sum), qkv_grad = lax.scan(per_head, start, (qkv_weight, out_weight, attended_grad))
    mixed = mixed_sum.astype(jnp.bfloat16).reshape(LEV, LAT, LON, D)
    latent_grad = latent_sum.astype(jnp.bfloat16).reshape(LEV, LAT, LON, D)
    return mixed, latent_grad, qkv_grad
```

```python
import functools

import jax
import jax.numpy as jnp
from jax import lax
from jax.experimental import pallas as pl
from jax.experimental.pallas import tpu as pltpu
from jax.sharding import Mesh, PartitionSpec as P

HD = 64
RANKS = 16
TOK = 72
HEAD = ("z", "yl")
LON = ("x", "yh", "core")
F32 = jnp.float32
BF16 = jnp.bfloat16


def dot_nt(a, b):
    return lax.dot_general(a, b, (((1,), (1,)), ((), ())), preferred_element_type=F32)


def dot_nn(a, b):
    return lax.dot_general(a, b, (((1,), (0,)), ((), ())), preferred_element_type=F32)


def dot_tn(a, b):
    return lax.dot_general(a, b, (((0,), (0,)), ((), ())), preferred_element_type=F32)


def call(body, outs, scratch=(), smem=(), n_in=1, flops=0, moved=0):
    specs = [
        pl.BlockSpec(memory_space=pltpu.SMEM if i in smem else pltpu.VMEM) for i in range(n_in)
    ]
    return pl.pallas_call(
        body,
        out_shape=[jax.ShapeDtypeStruct(s, d) for s, d in outs],
        in_specs=specs,
        out_specs=[pl.BlockSpec(memory_space=pltpu.VMEM) for _ in outs],
        scratch_shapes=list(scratch),
        cost_estimate=pl.CostEstimate(flops=flops, bytes_accessed=moved, transcendentals=0),
        compiler_params=pltpu.CompilerParams(vmem_limit_bytes=56 << 20),
    )


def low_half(shape):
    return lax.broadcasted_iota(jnp.int32, shape, len(shape) - 2) % 8 < 4


def pack_pair(value):
    groups = value.reshape(2, 72, 8, 128)
    first, second = groups[0], groups[1]
    low = low_half(first.shape)
    west = jnp.where(low, first, pltpu.roll(second, 4, 1))
    east = jnp.where(low, pltpu.roll(first, 4, 1), second)
    return west.reshape(8, TOK, 128), east.reshape(8, TOK, 128)


def unpack_pair(west, east):
    west = west.reshape(72, 8, 128)
    east = east.reshape(72, 8, 128)
    low = low_half(west.shape)
    first = jnp.where(low, west, pltpu.roll(east, 4, 1))
    second = jnp.where(low, pltpu.roll(west, 4, 1), east)
    return first.reshape(8, TOK, 128), second.reshape(8, TOK, 128)


def token_grad_kernel(grad_ref, weight_ref, out_ref):
    for pair in range(RANKS // 2):
        rows = weight_ref[2 * pair : 2 * pair + 2].reshape(2 * HD, -1)
        both = dot_nt(grad_ref[...], rows).astype(BF16)
        out_ref[2 * pair] = both[:, :HD]
        out_ref[2 * pair + 1] = both[:, HD:]


def project_kernel(table_ref, tokens_ref, weight_ref, kv_ref, q_ref, west_ref, east_ref, kv32):
    weight = weight_ref[...]
    for chunk in range(4):
        rows = tokens_ref[chunk * 288 : (chunk + 1) * 288, :]
        proj = dot_nt(rows, weight).astype(BF16).astype(F32)
        for part in range(4):
            rank = table_ref[chunk * 4 + part]
            piece = proj[part * TOK : (part + 1) * TOK]
            kv32[rank] = piece[:, :128]
            kv_ref[rank] = piece[:, :128].astype(BF16)
            q_ref[rank] = piece[:, 128:].astype(BF16)
    west, east = pack_pair(kv32[...])
    west_ref[...] = west.astype(BF16)
    east_ref[...] = east.astype(BF16)


def attend_kernel(
    kv_ref, q_ref, grad_ref, from_e_ref, from_w_ref,
    out_ref, dq_ref, dkv_ref, to_e_ref, to_w_ref,
    keys, halo, dhalo,
):
    scale = HD ** (-0.5)
    keys[...] = kv_ref[...].astype(F32)
    first, second = unpack_pair(from_e_ref[...].astype(F32), from_w_ref[...].astype(F32))
    halo[0:8] = first
    halo[8:16] = second
    zeros = jnp.zeros((2 * TOK, HD), F32)
    windows = RANKS // 2
    for w in range(windows):
        lo, hi = max(2 * w - 1, 0), min(2 * w + 3, RANKS)
        count = (hi - lo) * TOK
        query = q_ref[2 * w : 2 * w + 2].astype(F32).reshape(2 * TOK, HD) * scale
        outer = grad_ref[2 * w : 2 * w + 2].astype(F32).reshape(2 * TOK, HD)
        lhs = jnp.concatenate(
            [
                jnp.concatenate([query, zeros], axis=1),
                jnp.concatenate([zeros, outer], axis=1),
            ],
            axis=0,
        ).astype(BF16)
        pairs = jnp.concatenate(
            [keys[lo:hi].reshape(count, 128), halo[lo:hi].reshape(count, 128)], axis=0
        ).astype(BF16)
        both = dot_nt(lhs, pairs)
        score, prob_grad = both[: 2 * TOK], both[2 * TOK :]
        powers = jnp.exp(score - jnp.max(score, axis=-1, keepdims=True))
        probs = powers * (1.0 / jnp.sum(powers, axis=-1, keepdims=True))
        centre = jnp.sum(probs * prob_grad, axis=-1, keepdims=True)
        score_grad = (probs * (prob_grad - centre)).astype(BF16)
        stack = jnp.concatenate([score_grad, probs.astype(BF16)], axis=0)
        mixed = dot_nn(stack, pairs)
        dq_ref[2 * w : 2 * w + 2] = (mixed[: 2 * TOK, :HD] * scale).reshape(2, TOK, HD)
        out_ref[2 * w : 2 * w + 2] = mixed[2 * TOK :, HD:].reshape(2, TOK, HD).astype(BF16)
        grads = dot_tn(stack, lhs)
        own = grads[:count].reshape(hi - lo, TOK, 128)
        side = grads[count:].reshape(hi - lo, TOK, 128)
        for i, rank in enumerate(range(lo, hi)):
            seen = w > 0 and rank <= 2 * w
            if seen:
                dkv_ref[rank] += own[i]
                dhalo[rank] += side[i]
            else:
                dkv_ref[rank] = own[i]
                dhalo[rank] = side[i]
    to_e, to_w = pack_pair(dhalo[...])
    to_e_ref[...] = to_e.astype(BF16)
    to_w_ref[...] = to_w.astype(BF16)


def combine_kernel(
    dq_ref, dkv_ref, got_w_ref, got_e_ref, weight_ref, share_ref, pg_ref, pg32
):
    first, second = unpack_pair(got_w_ref[...].astype(F32), got_e_ref[...].astype(F32))
    for half, add in ((0, first), (1, second)):
        span = slice(8 * half, 8 * half + 8)
        pg32[span, :, 0:128] = dkv_ref[span] + add
        pg32[span, :, 128:192] = dq_ref[span]
    weight = weight_ref[...]
    for chunk in range(4):
        rows = pg32[4 * chunk : 4 * chunk + 4].reshape(4 * TOK, 3 * HD).astype(BF16)
        pg_ref[4 * chunk : 4 * chunk + 4] = rows.reshape(4, TOK, 3 * HD)
        part = dot_nn(rows, weight)
        share_ref[4 * chunk : 4 * chunk + 4] = part.reshape(4, TOK, -1).astype(BF16)


def weight_grad_kernel(table_ref, tokens_ref, pg_ref, piece_ref):
    total = None
    for chunk in range(4):
        rows = jnp.concatenate(
            [pg_ref[table_ref[4 * chunk + i]].astype(F32) for i in range(4)], axis=0
        ).astype(BF16)
        part = dot_tn(rows, tokens_ref[chunk * 288 : (chunk + 1) * 288, :])
        total = part if total is None else total + part
    total = jnp.concatenate([total[128:192], total[0:128]], axis=0).astype(BF16)
    for g in range(4):
        for j in range(8):
            piece_ref[8 * g + j] = total[48 * g : 48 * g + 48, 128 * j : 128 * j + 128]


def mix_kernel(att_ref, weight_ref, out_ref):
    rows = jnp.concatenate([att_ref[h] for h in range(RANKS)], axis=1)
    out_ref[...] = dot_nn(rows, weight_ref[...]).astype(BF16)


def shift(value, axis, size, distance):
    return lax.ppermute(value, axis, [(i, (i + distance) % size) for i in range(size)])


def exchange(value, axis):
    return lax.all_to_all(value, axis, 0, 0, tiled=True)


def body(latents, out_grad, qkv_weight, out_weight):
    width = latents.shape[-1]
    z, yl = lax.axis_index("z"), lax.axis_index("yl")
    mine = latents.reshape(TOK, width)
    blocks = [mine] + [shift(mine, "z", 8, d) for d in (1, 7, 2, 6, 3, 5, 4)]
    blocks = blocks + [shift(b, "yl", 2, 1) for b in blocks]
    distance = jnp.array([0, 1, 7, 2, 6, 3, 5, 4], jnp.int32)
    table = 2 * ((z - distance) % 8)
    table = jnp.concatenate([table + yl, table + 1 - yl]).astype(jnp.int32)

    (token_grad,) = call(
        token_grad_kernel, [((RANKS, TOK, HD), BF16)], n_in=2, flops=2 * TOK * width * width
    )(out_grad.reshape(TOK, width), out_weight)
    band_grad = exchange(token_grad, HEAD)

    turned = jnp.swapaxes(qkv_weight[0], 0, 1)
    turned = jnp.concatenate([turned[HD:], turned[:HD]], axis=0)
    tokens = jnp.concatenate(blocks, axis=0)
    kv, query, to_west, to_east = call(
        project_kernel,
        [
            ((RANKS, TOK, 128), BF16),
            ((RANKS, TOK, HD), BF16),
            ((8, TOK, 128), BF16),
            ((8, TOK, 128), BF16),
        ],
        scratch=[pltpu.VMEM((RANKS, TOK, 128), F32)],
        smem=(0,),
        n_in=3,
        flops=2 * 1152 * 192 * width,
    )(table, tokens, turned)
    from_east = shift(to_west, LON, 32, -1)
    from_west = shift(to_east, LON, 32, 1)
    attended, dq, dkv, grad_east, grad_west = call(
        attend_kernel,
        [
            ((RANKS, TOK, HD), BF16),
            ((RANKS, TOK, HD), F32),
            ((RANKS, TOK, 128), F32),
            ((8, TOK, 128), BF16),
            ((8, TOK, 128), BF16),
        ],
        scratch=[pltpu.VMEM((RANKS, TOK, 128), F32)] * 3,
        n_in=5,
        flops=8 * 6 * 2 * 144 * 576 * 128,
    )(kv, query, band_grad, from_east, from_west)
    got_west = shift(grad_east, LON, 32, 1)
    got_east = shift(grad_west, LON, 32, -1)
    token_att = exchange(attended, HEAD)

    share, pg = call(
        combine_kernel,
        [((RANKS, TOK, width), BF16), ((RANKS, TOK, 3 * HD), BF16)],
        scratch=[pltpu.VMEM((RANKS, TOK, 3 * HD), F32)],
        n_in=5,
        flops=2 * 1152 * 192 * width,
    )(dq, dkv, got_west, got_east, turned)
    shares = exchange(share, HEAD)
    (pieces,) = call(
        weight_grad_kernel, [((32, 48, 128), BF16)], smem=(0,), n_in=3, flops=2 * 1152 * 192 * width
    )(table, tokens, pg)
    pieces = exchange(pieces, LON)
    summed = jnp.sum(pieces.astype(F32), axis=0).astype(BF16)
    copies = exchange(jnp.broadcast_to(summed[None], (32, 48, 128)), LON)
    (mixed,) = call(mix_kernel, [((TOK, width), BF16)], n_in=2, flops=2 * TOK * width * width)(
        token_att, out_weight.reshape(width, width)
    )
    latent_grad = jnp.sum(shares.astype(F32), axis=0).astype(BF16)
    grad = copies.reshape(4, 8, 48, 128).transpose(0, 2, 1, 3).reshape(3 * HD, width)
    qkv_grad = jnp.swapaxes(grad, 0, 1).astype(F32)[None]
    return mixed.reshape(latents.shape), latent_grad.reshape(latents.shape), qkv_grad


def solution(mesh):
    split = Mesh(mesh.devices.reshape(4, 4, 2, 8, 2), LON + HEAD)
    rows = P(None, HEAD, LON, None)
    return jax.shard_map(
        body,
        mesh=split,
        in_specs=(rows, rows, P(HEAD, None, None), P()),
        out_specs=(rows, rows, P(HEAD, None, None)),
        check_vma=False,
    )
```

```python
import jax
import jax.numpy as jnp
from jax import lax
from jax.experimental import pallas as pl
from jax.experimental.pallas import tpu as pltpu
from jax.sharding import Mesh, PartitionSpec as P

HD = 64
RANKS = 16
TOK = 72
HEAD = ("z", "yl")
LON = ("x", "yh", "core")
F32 = jnp.float32
BF16 = jnp.bfloat16


def dot_nt(a, b):
    return lax.dot_general(a, b, (((1,), (1,)), ((), ())), preferred_element_type=F32)


def dot_nn(a, b):
    return lax.dot_general(a, b, (((1,), (0,)), ((), ())), preferred_element_type=F32)


def dot_tn(a, b):
    return lax.dot_general(a, b, (((0,), (0,)), ((), ())), preferred_element_type=F32)


def call(body, outs, scratch=(), smem=(), n_in=1, flops=0, moved=0):
    specs = [
        pl.BlockSpec(memory_space=pltpu.SMEM if i in smem else pltpu.VMEM) for i in range(n_in)
    ]
    return pl.pallas_call(
        body,
        out_shape=[jax.ShapeDtypeStruct(s, d) for s, d in outs],
        in_specs=specs,
        out_specs=[pl.BlockSpec(memory_space=pltpu.VMEM) for _ in outs],
        scratch_shapes=list(scratch),
        cost_estimate=pl.CostEstimate(flops=flops, bytes_accessed=moved, transcendentals=0),
        compiler_params=pltpu.CompilerParams(vmem_limit_bytes=56 << 20),
    )


def low_half(shape):
    return lax.broadcasted_iota(jnp.int32, shape, len(shape) - 2) % 8 < 4


def pack_pair(value):
    half = value.shape[0] // 2
    groups = value.reshape(2, half * TOK // 8, 8, 128)
    first, second = groups[0], groups[1]
    low = low_half(first.shape)
    west = jnp.where(low, first, pltpu.roll(second, 4, 1))
    east = jnp.where(low, pltpu.roll(first, 4, 1), second)
    return west.reshape(half, TOK, 128), east.reshape(half, TOK, 128)


def unpack_pair(west, east):
    half = west.shape[0]
    west = west.reshape(half * TOK // 8, 8, 128)
    east = east.reshape(half * TOK // 8, 8, 128)
    low = low_half(west.shape)
    first = jnp.where(low, west, pltpu.roll(east, 4, 1))
    second = jnp.where(low, pltpu.roll(west, 4, 1), east)
    return first.reshape(half, TOK, 128), second.reshape(half, TOK, 128)


def fold_rows(value):
    rest = jnp.concatenate([value[40:], jnp.zeros((8, HD), F32)], axis=0)
    return jnp.concatenate([value[:40], rest], axis=1)


def unfold_rows(value):
    return jnp.concatenate([value[:, :HD], value[:32, HD:]], axis=0)


def turned(ref):
    return jnp.concatenate([ref[HD : 3 * HD], ref[0:HD]], axis=0)


def token_grad_kernel(grad_ref, weight_ref, out_ref):
    for pair in range(RANKS // 2):
        rows = weight_ref[2 * pair : 2 * pair + 2].reshape(2 * HD, -1)
        both = dot_nt(grad_ref[...], rows)
        out_ref[2 * pair] = fold_rows(both[:, :HD]).astype(BF16)
        out_ref[2 * pair + 1] = fold_rows(both[:, HD:]).astype(BF16)


def project_kernel(
    table_ref, tokens_ref, own_ref, other_ref,
    kv_ref, q_ref, swap_ref, west_ref, east_ref, west2_ref, east2_ref,
    kv32, kv32b,
):
    own, other = turned(own_ref), turned(other_ref)
    for chunk in range(2):
        rows = tokens_ref[chunk * 288 : (chunk + 1) * 288, :]
        proj = dot_nt(rows, own).astype(BF16).astype(F32)
        proj2 = dot_nt(rows, other).astype(BF16).astype(F32)
        for part in range(4):
            row = table_ref[chunk * 4 + part]
            piece = proj[part * TOK : (part + 1) * TOK]
            kv32[row] = piece[:, :128]
            kv_ref[row] = piece[:, :128].astype(BF16)
            q_ref[row] = piece[:, 128:].astype(BF16)
            piece = proj2[part * TOK : (part + 1) * TOK]
            kv32b[row] = piece[:, :128]
            swap_ref[row] = piece.astype(BF16)
    west, east = pack_pair(kv32[...])
    west_ref[...] = west.astype(BF16)
    east_ref[...] = east.astype(BF16)
    west, east = pack_pair(kv32b[...])
    west2_ref[...] = west.astype(BF16)
    east2_ref[...] = east.astype(BF16)


def attend_kernel(
    place_ref, kv_ref, q_ref, swapped_ref, grad_ref, from_e_ref, from_w_ref, from_e2_ref, from_w2_ref,
    out_ref, dq_ref, dkv_ref, to_e_ref, to_w_ref,
    keys, queries, halo, dhalo,
):
    scale = HD ** (-0.5)
    yl = place_ref[0]
    side = unpack_pair(from_e_ref[...].astype(F32), from_w_ref[...].astype(F32))
    side2 = unpack_pair(from_e2_ref[...].astype(F32), from_w2_ref[...].astype(F32))
    for row in range(8):
        mine, theirs = 2 * row + yl, 2 * row + 1 - yl
        keys[mine] = kv_ref[row].astype(F32)
        queries[mine] = q_ref[row].astype(F32)
        both = swapped_ref[row].astype(F32)
        keys[theirs] = both[:, :128]
        queries[theirs] = both[:, 128:]
        halo[mine] = side[row // 4][row % 4]
        halo[theirs] = side2[row // 4][row % 4]
    zeros = jnp.zeros((2 * TOK, HD), F32)
    windows = RANKS // 2
    for w in range(windows):
        lo, hi = max(2 * w - 1, 0), min(2 * w + 3, RANKS)
        count = (hi - lo) * TOK
        query = queries[2 * w : 2 * w + 2].reshape(2 * TOK, HD) * scale
        outer = jnp.concatenate(
            [unfold_rows(grad_ref[2 * w + i].astype(F32)) for i in range(2)], axis=0
        )
        lhs = jnp.concatenate(
            [
                jnp.concatenate([query, zeros], axis=1),
                jnp.concatenate([zeros, outer], axis=1),
            ],
            axis=0,
        ).astype(BF16)
        pairs = jnp.concatenate(
            [keys[lo:hi].reshape(count, 128), halo[lo:hi].reshape(count, 128)], axis=0
        ).astype(BF16)
        both = dot_nt(lhs, pairs)
        score, prob_grad = both[: 2 * TOK], both[2 * TOK :]
        powers = jnp.exp(score - jnp.max(score, axis=-1, keepdims=True))
        probs = powers * (1.0 / jnp.sum(powers, axis=-1, keepdims=True))
        centre = jnp.sum(probs * prob_grad, axis=-1, keepdims=True)
        score_grad = (probs * (prob_grad - centre)).astype(BF16)
        stack = jnp.concatenate([score_grad, probs.astype(BF16)], axis=0)
        mixed = dot_nn(stack, pairs)
        dq_ref[2 * w : 2 * w + 2] = (mixed[: 2 * TOK, :HD] * scale).reshape(2, TOK, HD)
        for i in range(2):
            rows = mixed[(2 + i) * TOK : (3 + i) * TOK, HD:]
            out_ref[2 * w + i] = fold_rows(rows).astype(BF16)
        grads = dot_tn(stack, lhs)
        own = grads[:count].reshape(hi - lo, TOK, 128)
        side = grads[count:].reshape(hi - lo, TOK, 128)
        for i, rank in enumerate(range(lo, hi)):
            seen = w > 0 and rank <= 2 * w
            if seen:
                dkv_ref[rank] += own[i]
                dhalo[rank] += side[i]
            else:
                dkv_ref[rank] = own[i]
                dhalo[rank] = side[i]
    to_e, to_w = pack_pair(dhalo[...])
    to_e_ref[...] = to_e.astype(BF16)
    to_w_ref[...] = to_w.astype(BF16)


def combine_kernel(
    place_ref, dq_ref, dkv_ref, got_w_ref, got_e_ref, pg_ref, mine_ref, swap_ref, pg32
):
    yl = place_ref[0]
    first, second = unpack_pair(got_w_ref[...].astype(F32), got_e_ref[...].astype(F32))
    for half, add in ((0, first), (1, second)):
        span = slice(8 * half, 8 * half + 8)
        pg32[span, :, 0:128] = dkv_ref[span] + add
        pg32[span, :, 128:192] = dq_ref[span]
    pg_ref[...] = pg32[...].astype(BF16)
    for row in range(8):
        mine_ref[row] = pg32[2 * row + yl].astype(BF16)
        swap_ref[row] = pg32[2 * row + 1 - yl].astype(BF16)


def share_kernel(table_ref, mine_ref, got_ref, own_ref, other_ref, *out_refs):
    own, other = turned(own_ref), turned(other_ref)
    for chunk in range(2):
        picks = [table_ref[4 * chunk + i] for i in range(4)]
        rows = jnp.concatenate([mine_ref[p].astype(F32) for p in picks], axis=0).astype(BF16)
        rows2 = jnp.concatenate([got_ref[p].astype(F32) for p in picks], axis=0).astype(BF16)
        part = dot_nn(rows, own) + dot_nn(rows2, other)
        for i in range(4):
            out_refs[4 * chunk + i][...] = part[i * TOK : (i + 1) * TOK].astype(BF16)


def weight_grad_kernel(table_ref, tokens_ref, tokens2_ref, pg_ref, piece_ref):
    total = None
    for chunk in range(4):
        rows = jnp.concatenate(
            [pg_ref[table_ref[4 * chunk + i]].astype(F32) for i in range(4)], axis=0
        ).astype(BF16)
        source = tokens_ref if chunk < 2 else tokens2_ref
        span = slice((chunk % 2) * 288, (chunk % 2) * 288 + 288)
        part = dot_tn(rows, source[span, :])
        total = part if total is None else total + part
    total = jnp.concatenate([total[128:192], total[0:128]], axis=0).astype(BF16)
    for g in range(4):
        for j in range(8):
            piece_ref[8 * g + j] = total[48 * g : 48 * g + 48, 128 * j : 128 * j + 128]


def mix_kernel(att_ref, weight_ref, out_ref):
    rows = [unfold_rows(att_ref[h].astype(F32)) for h in range(RANKS)]
    rows = jnp.concatenate(rows, axis=1).astype(BF16)
    out_ref[...] = dot_nn(rows, weight_ref[...]).astype(BF16)


def shift(value, axis, size, distance):
    return lax.ppermute(value, axis, [(i, (i + distance) % size) for i in range(size)])


def exchange(value, axis):
    return lax.all_to_all(value, axis, 0, 0, tiled=True)


def step(latents, out_grad, qkv_weight, out_weight):
    width = latents.shape[-1]
    z, yl = lax.axis_index("z"), lax.axis_index("yl")
    mine = latents.reshape(TOK, width)
    own = jnp.swapaxes(qkv_weight[0], 0, 1)
    d1, d7, d2, d6 = (shift(mine, "z", 8, d) for d in (1, 7, 2, 6))
    other = shift(own, "yl", 2, 1)
    d3, d5 = shift(d2, "z", 8, 1), shift(d6, "z", 8, -1)
    d4 = shift(d2, "z", 8, 2)
    tokens = jnp.concatenate([mine, d1, d7, d2, d6, d3, d5, d4], axis=0)
    distance = jnp.array([0, 1, 7, 2, 6, 3, 5, 4], jnp.int32)
    rows = ((z - distance) % 8).astype(jnp.int32)
    place = yl.astype(jnp.int32).reshape(1)

    (token_grad,) = call(
        token_grad_kernel, [((RANKS, 40, 128), BF16)], n_in=2, flops=2 * TOK * width * width
    )(out_grad.reshape(TOK, width), out_weight)
    band_grad = exchange(token_grad, HEAD)

    kv, query, swap, to_w, to_e, to_w2, to_e2 = call(
        project_kernel,
        [((8, TOK, 128), BF16), ((8, TOK, HD), BF16), ((8, TOK, 3 * HD), BF16)]
        + [((4, TOK, 128), BF16)] * 4,
        scratch=[pltpu.VMEM((8, TOK, 128), F32)] * 2,
        smem=(0,),
        n_in=4,
        flops=2 * 1152 * 192 * width,
    )(rows, tokens, own, other)
    from_e = shift(to_w, LON, 32, -1)
    from_w = shift(to_e, LON, 32, 1)
    from_e2 = lax.ppermute(to_w2, LON + ("yl",), across(-1))
    from_w2 = lax.ppermute(to_e2, LON + ("yl",), across(1))
    swapped = shift(swap, "yl", 2, 1)
    late, from_e, from_w, from_e2, from_w2, swapped = lax.optimization_barrier(
        (tokens, from_e, from_w, from_e2, from_w2, swapped)
    )
    tokens2 = shift(late, "yl", 2, 1)
    attended, dq, dkv, grad_east, grad_west = call(
        attend_kernel,
        [
            ((RANKS, 40, 128), BF16),
            ((RANKS, TOK, HD), F32),
            ((RANKS, TOK, 128), F32),
            ((8, TOK, 128), BF16),
            ((8, TOK, 128), BF16),
        ],
        scratch=[
            pltpu.VMEM((RANKS, TOK, 128), F32),
            pltpu.VMEM((RANKS, TOK, HD), F32),
            pltpu.VMEM((RANKS, TOK, 128), F32),
            pltpu.VMEM((RANKS, TOK, 128), F32),
        ],
        smem=(0,),
        n_in=9,
        flops=8 * 6 * 2 * 144 * 576 * 128,
    )(place, kv, query, swapped, band_grad, from_e, from_w, from_e2, from_w2)
    got_west = shift(grad_east, LON, 32, 1)
    got_east = shift(grad_west, LON, 32, -1)
    token_att = exchange(attended, HEAD)

    pg, pg_mine, pg_swap = call(
        combine_kernel,
        [((RANKS, TOK, 3 * HD), BF16), ((8, TOK, 3 * HD), BF16), ((8, TOK, 3 * HD), BF16)],
        scratch=[pltpu.VMEM((RANKS, TOK, 3 * HD), F32)],
        smem=(0,),
        n_in=5,
        flops=1 << 20,
    )(place, dq, dkv, got_west, got_east)
    pg_got = shift(pg_swap, "yl", 2, 1)
    (pieces,) = call(
        weight_grad_kernel,
        [((32, 48, 128), BF16)],
        smem=(0,),
        n_in=4,
        flops=2 * 1152 * 192 * width,
    )(
        jnp.concatenate([2 * rows + yl, 2 * rows + 1 - yl]).astype(jnp.int32),
        tokens, tokens2, pg,
    )
    pieces = exchange(pieces, LON)
    reach = (4, 3, 5, 2, 6, 1, 7, 0)
    shares = call(
        share_kernel,
        [((TOK, width), BF16)] * 8,
        smem=(0,),
        n_in=5,
        flops=2 * 576 * 384 * width,
    )(((z + jnp.array(reach, jnp.int32)) % 8).astype(jnp.int32), pg_mine, pg_got, own, other)
    shares = [shift(s, "z", 8, d) if d else s for s, d in zip(shares, reach)]
    summed = jnp.sum(pieces.astype(F32), axis=0).astype(BF16)
    copies = exchange(jnp.broadcast_to(summed[None], (32, 48, 128)), LON)
    (mixed,) = call(mix_kernel, [((TOK, width), BF16)], n_in=2, flops=2 * TOK * width * width)(
        token_att, out_weight.reshape(width, width)
    )
    latent_grad = sum(s.astype(F32) for s in shares).astype(BF16)
    grad = copies.reshape(4, 8, 48, 128).transpose(0, 2, 1, 3).reshape(3 * HD, width)
    qkv_grad = jnp.swapaxes(grad, 0, 1).astype(F32)[None]
    return mixed.reshape(latents.shape), latent_grad.reshape(latents.shape), qkv_grad


def across(distance):
    return [(2 * i + j, 2 * ((i + distance) % 32) + 1 - j) for i in range(32) for j in range(2)]


def solution(mesh):
    split = Mesh(mesh.devices.reshape(4, 4, 2, 8, 2), LON + HEAD)
    rows = P(None, HEAD, LON, None)
    return jax.shard_map(
        step,
        mesh=split,
        in_specs=(rows, rows, P(HEAD, None, None), P()),
        out_specs=(rows, rows, P(HEAD, None, None)),
        check_vma=False,
    )
```

```python
import jax
import jax.numpy as jnp
from jax import lax
from jax.experimental import pallas as pl
from jax.experimental.pallas import tpu as pltpu
from jax.sharding import Mesh, PartitionSpec as P

HD = 64
RANKS = 16
TOK = 72
HEAD = ("z", "yl")
LON = ("x", "yh", "core")
F32 = jnp.float32
BF16 = jnp.bfloat16


def dot_nt(a, b):
    return lax.dot_general(a, b, (((1,), (1,)), ((), ())), preferred_element_type=F32)


def dot_nn(a, b):
    return lax.dot_general(a, b, (((1,), (0,)), ((), ())), preferred_element_type=F32)


def dot_tn(a, b):
    return lax.dot_general(a, b, (((0,), (0,)), ((), ())), preferred_element_type=F32)


def call(body, outs, scratch=(), smem=(), n_in=1, flops=0, moved=0):
    specs = [
        pl.BlockSpec(memory_space=pltpu.SMEM if i in smem else pltpu.VMEM) for i in range(n_in)
    ]
    return pl.pallas_call(
        body,
        out_shape=[jax.ShapeDtypeStruct(s, d) for s, d in outs],
        in_specs=specs,
        out_specs=[pl.BlockSpec(memory_space=pltpu.VMEM) for _ in outs],
        scratch_shapes=list(scratch),
        cost_estimate=pl.CostEstimate(flops=flops, bytes_accessed=moved, transcendentals=0),
        compiler_params=pltpu.CompilerParams(vmem_limit_bytes=56 << 20),
    )


def low_half(shape):
    return lax.broadcasted_iota(jnp.int32, shape, len(shape) - 2) % 8 < 4


def pack_pair(value):
    half = value.shape[0] // 2
    groups = value.reshape(2, half * TOK // 8, 8, 128)
    first, second = groups[0], groups[1]
    low = low_half(first.shape)
    west = jnp.where(low, first, pltpu.roll(second, 4, 1))
    east = jnp.where(low, pltpu.roll(first, 4, 1), second)
    return west.reshape(half, TOK, 128), east.reshape(half, TOK, 128)


def unpack_pair(west, east):
    half = west.shape[0]
    west = west.reshape(half * TOK // 8, 8, 128)
    east = east.reshape(half * TOK // 8, 8, 128)
    low = low_half(west.shape)
    first = jnp.where(low, west, pltpu.roll(east, 4, 1))
    second = jnp.where(low, pltpu.roll(west, 4, 1), east)
    return first.reshape(half, TOK, 128), second.reshape(half, TOK, 128)


def fold_rows(value):
    rest = jnp.concatenate([value[40:], jnp.zeros((8, HD), F32)], axis=0)
    return jnp.concatenate([value[:40], rest], axis=1)


def unfold_rows(value):
    return jnp.concatenate([value[:, :HD], value[:32, HD:]], axis=0)


def turned(ref):
    return jnp.concatenate([ref[HD : 3 * HD], ref[0:HD]], axis=0)


def token_grad_kernel(grad_ref, weight_ref, out_ref):
    for pair in range(RANKS // 2):
        rows = weight_ref[2 * pair : 2 * pair + 2].reshape(2 * HD, -1)
        both = dot_nt(grad_ref[...], rows)
        out_ref[2 * pair] = fold_rows(both[:, :HD]).astype(BF16)
        out_ref[2 * pair + 1] = fold_rows(both[:, HD:]).astype(BF16)


def project_kernel(
    table_ref, tokens_ref, own_ref, other_ref,
    kv_ref, q_ref, swap_ref, west_ref, east_ref, west2_ref, east2_ref,
    kv32, kv32b,
):
    own, other = turned(own_ref), turned(other_ref)
    for chunk in range(2):
        rows = tokens_ref[chunk * 288 : (chunk + 1) * 288, :]
        proj = dot_nt(rows, own).astype(BF16).astype(F32)
        proj2 = dot_nt(rows, other).astype(BF16).astype(F32)
        for part in range(4):
            row = table_ref[chunk * 4 + part]
            piece = proj[part * TOK : (part + 1) * TOK]
            kv32[row] = piece[:, :128]
            kv_ref[row] = piece[:, :128].astype(BF16)
            q_ref[row] = piece[:, 128:].astype(BF16)
            piece = proj2[part * TOK : (part + 1) * TOK]
            kv32b[row] = piece[:, :128]
            swap_ref[row] = piece.astype(BF16)
    west, east = pack_pair(kv32[...])
    west_ref[...] = west.astype(BF16)
    east_ref[...] = east.astype(BF16)
    west, east = pack_pair(kv32b[...])
    west2_ref[...] = west.astype(BF16)
    east2_ref[...] = east.astype(BF16)


def attend_kernel(
    place_ref, kv_ref, q_ref, swapped_ref, grad_ref, from_e_ref, from_w_ref, from_e2_ref, from_w2_ref,
    out_ref, dq_ref, dkv_ref, to_e_ref, to_w_ref,
    keys, queries, halo, dhalo,
):
    scale = HD ** (-0.5)
    yl = place_ref[0]
    side = unpack_pair(from_e_ref[...].astype(F32), from_w_ref[...].astype(F32))
    side2 = unpack_pair(from_e2_ref[...].astype(F32), from_w2_ref[...].astype(F32))
    for row in range(8):
        mine, theirs = 2 * row + yl, 2 * row + 1 - yl
        keys[mine] = kv_ref[row].astype(F32)
        queries[mine] = q_ref[row].astype(F32)
        both = swapped_ref[row].astype(F32)
        keys[theirs] = both[:, :128]
        queries[theirs] = both[:, 128:]
        halo[mine] = side[row // 4][row % 4]
        halo[theirs] = side2[row // 4][row % 4]
    zeros = jnp.zeros((2 * TOK, HD), F32)
    windows = RANKS // 2
    for w in range(windows):
        lo, hi = max(2 * w - 1, 0), min(2 * w + 3, RANKS)
        count = (hi - lo) * TOK
        query = queries[2 * w : 2 * w + 2].reshape(2 * TOK, HD) * scale
        outer = jnp.concatenate(
            [unfold_rows(grad_ref[2 * w + i].astype(F32)) for i in range(2)], axis=0
        )
        lhs = jnp.concatenate(
            [
                jnp.concatenate([query, zeros], axis=1),
                jnp.concatenate([zeros, outer], axis=1),
            ],
            axis=0,
        ).astype(BF16)
        pairs = jnp.concatenate(
            [keys[lo:hi].reshape(count, 128), halo[lo:hi].reshape(count, 128)], axis=0
        ).astype(BF16)
        both = dot_nt(lhs, pairs)
        score, prob_grad = both[: 2 * TOK], both[2 * TOK :]
        powers = jnp.exp(score - jnp.max(score, axis=-1, keepdims=True))
        probs = powers * (1.0 / jnp.sum(powers, axis=-1, keepdims=True))
        centre = jnp.sum(probs * prob_grad, axis=-1, keepdims=True)
        score_grad = (probs * (prob_grad - centre)).astype(BF16)
        stack = jnp.concatenate([score_grad, probs.astype(BF16)], axis=0)
        mixed = dot_nn(stack, pairs)
        dq_ref[2 * w : 2 * w + 2] = (mixed[: 2 * TOK, :HD] * scale).reshape(2, TOK, HD)
        for i in range(2):
            rows = mixed[(2 + i) * TOK : (3 + i) * TOK, HD:]
            out_ref[2 * w + i] = fold_rows(rows).astype(BF16)
        grads = dot_tn(stack, lhs)
        own = grads[:count].reshape(hi - lo, TOK, 128)
        side = grads[count:].reshape(hi - lo, TOK, 128)
        for i, rank in enumerate(range(lo, hi)):
            seen = w > 0 and rank <= 2 * w
            if seen:
                dkv_ref[rank] += own[i]
                dhalo[rank] += side[i]
            else:
                dkv_ref[rank] = own[i]
                dhalo[rank] = side[i]
    to_e, to_w = pack_pair(dhalo[...])
    to_e_ref[...] = to_e.astype(BF16)
    to_w_ref[...] = to_w.astype(BF16)


def combine_kernel(
    place_ref, dq_ref, dkv_ref, got_w_ref, got_e_ref, pg_ref, mine_ref, swap_ref, pg32
):
    yl = place_ref[0]
    first, second = unpack_pair(got_w_ref[...].astype(F32), got_e_ref[...].astype(F32))
    for half, add in ((0, first), (1, second)):
        span = slice(8 * half, 8 * half + 8)
        pg32[span, :, 0:128] = dkv_ref[span] + add
        pg32[span, :, 128:192] = dq_ref[span]
    pg_ref[...] = pg32[...].astype(BF16)
    for row in range(8):
        mine_ref[row] = pg32[2 * row + yl].astype(BF16)
        swap_ref[row] = pg32[2 * row + 1 - yl].astype(BF16)


def share_kernel(table_ref, mine_ref, got_ref, own_ref, other_ref, *out_refs):
    own, other = turned(own_ref), turned(other_ref)
    for chunk in range(2):
        picks = [table_ref[4 * chunk + i] for i in range(4)]
        rows = jnp.concatenate([mine_ref[p].astype(F32) for p in picks], axis=0).astype(BF16)
        rows2 = jnp.concatenate([got_ref[p].astype(F32) for p in picks], axis=0).astype(BF16)
        part = dot_nn(rows, own) + dot_nn(rows2, other)
        for i in range(4):
            out_refs[4 * chunk + i][...] = part[i * TOK : (i + 1) * TOK].astype(BF16)


def weight_grad_kernel(table_ref, tokens_ref, tokens2_ref, pg_ref, piece_ref):
    total = None
    for chunk in range(4):
        rows = jnp.concatenate(
            [pg_ref[table_ref[4 * chunk + i]].astype(F32) for i in range(4)], axis=0
        ).astype(BF16)
        source = tokens_ref if chunk < 2 else tokens2_ref
        span = slice((chunk % 2) * 288, (chunk % 2) * 288 + 288)
        part = dot_tn(rows, source[span, :])
        total = part if total is None else total + part
    total = jnp.concatenate([total[128:192], total[0:128]], axis=0).astype(BF16)
    for g in range(4):
        for j in range(8):
            piece_ref[8 * g + j] = total[48 * g : 48 * g + 48, 128 * j : 128 * j + 128]


def mix_kernel(att_ref, weight_ref, out_ref):
    rows = [unfold_rows(att_ref[h].astype(F32)) for h in range(RANKS)]
    rows = jnp.concatenate(rows, axis=1).astype(BF16)
    out_ref[...] = dot_nn(rows, weight_ref[...]).astype(BF16)


def shift(value, axis, size, distance):
    return lax.ppermute(value, axis, [(i, (i + distance) % size) for i in range(size)])


def exchange(value, axis):
    return lax.all_to_all(value, axis, 0, 0, tiled=True)


def step(latents, out_grad, qkv_weight, out_weight):
    width = latents.shape[-1]
    z, yl = lax.axis_index("z"), lax.axis_index("yl")
    mine = latents.reshape(TOK, width)
    own = jnp.swapaxes(qkv_weight[0], 0, 1)
    d1, d7, d2, d6 = (shift(mine, "z", 8, d) for d in (1, 7, 2, 6))
    other = shift(own, "yl", 2, 1)
    d3, d5 = shift(d2, "z", 8, 1), shift(d6, "z", 8, -1)
    d4 = shift(d2, "z", 8, 2)
    tokens = jnp.concatenate([mine, d1, d7, d2, d6, d3, d5, d4], axis=0)
    distance = jnp.array([0, 1, 7, 2, 6, 3, 5, 4], jnp.int32)
    rows = ((z - distance) % 8).astype(jnp.int32)
    place = yl.astype(jnp.int32).reshape(1)

    (token_grad,) = call(
        token_grad_kernel, [((RANKS, 40, 128), BF16)], n_in=2, flops=2 * TOK * width * width
    )(out_grad.reshape(TOK, width), out_weight)
    band_grad = exchange(token_grad, HEAD)

    kv, query, swap, to_w, to_e, to_w2, to_e2 = call(
        project_kernel,
        [((8, TOK, 128), BF16), ((8, TOK, HD), BF16), ((8, TOK, 3 * HD), BF16)]
        + [((4, TOK, 128), BF16)] * 4,
        scratch=[pltpu.VMEM((8, TOK, 128), F32)] * 2,
        smem=(0,),
        n_in=4,
        flops=2 * 1152 * 192 * width,
    )(rows, tokens, own, other)
    from_e = shift(to_w, LON, 32, -1)
    from_w = shift(to_e, LON, 32, 1)
    from_e2 = lax.ppermute(to_w2, LON + ("yl",), across(-1))
    from_w2 = lax.ppermute(to_e2, LON + ("yl",), across(1))
    swapped = shift(swap, "yl", 2, 1)
    tokens2 = shift(tokens, "yl", 2, 1)
    attended, dq, dkv, grad_east, grad_west = call(
        attend_kernel,
        [
            ((RANKS, 40, 128), BF16),
            ((RANKS, TOK, HD), F32),
            ((RANKS, TOK, 128), F32),
            ((8, TOK, 128), BF16),
            ((8, TOK, 128), BF16),
        ],
        scratch=[
            pltpu.VMEM((RANKS, TOK, 128), F32),
            pltpu.VMEM((RANKS, TOK, HD), F32),
            pltpu.VMEM((RANKS, TOK, 128), F32),
            pltpu.VMEM((RANKS, TOK, 128), F32),
        ],
        smem=(0,),
        n_in=9,
        flops=8 * 6 * 2 * 144 * 576 * 128,
    )(place, kv, query, swapped, band_grad, from_e, from_w, from_e2, from_w2)
    got_west = shift(grad_east, LON, 32, 1)
    got_east = shift(grad_west, LON, 32, -1)
    token_att = exchange(attended, HEAD)

    pg, pg_mine, pg_swap = call(
        combine_kernel,
        [((RANKS, TOK, 3 * HD), BF16), ((8, TOK, 3 * HD), BF16), ((8, TOK, 3 * HD), BF16)],
        scratch=[pltpu.VMEM((RANKS, TOK, 3 * HD), F32)],
        smem=(0,),
        n_in=5,
        flops=1 << 20,
    )(place, dq, dkv, got_west, got_east)
    pg_got = shift(pg_swap, "yl", 2, 1)
    (pieces,) = call(
        weight_grad_kernel,
        [((32, 48, 128), BF16)],
        smem=(0,),
        n_in=4,
        flops=2 * 1152 * 192 * width,
    )(
        jnp.concatenate([2 * rows + yl, 2 * rows + 1 - yl]).astype(jnp.int32),
        tokens, tokens2, pg,
    )
    pieces = exchange(pieces, LON)
    reach = (4, 3, 5, 2, 6, 1, 7, 0)
    shares = call(
        share_kernel,
        [((TOK, width), BF16)] * 8,
        smem=(0,),
        n_in=5,
        flops=2 * 576 * 384 * width,
    )(((z + jnp.array(reach, jnp.int32)) % 8).astype(jnp.int32), pg_mine, pg_got, own, other)
    shares = [shift(s, "z", 8, d) if d else s for s, d in zip(shares, reach)]
    summed = jnp.sum(pieces.astype(F32), axis=0).astype(BF16)
    copies = exchange(jnp.broadcast_to(summed[None], (32, 48, 128)), LON)
    (mixed,) = call(mix_kernel, [((TOK, width), BF16)], n_in=2, flops=2 * TOK * width * width)(
        token_att, out_weight.reshape(width, width)
    )
    latent_grad = sum(s.astype(F32) for s in shares).astype(BF16)
    grad = copies.reshape(4, 8, 48, 128).transpose(0, 2, 1, 3).reshape(3 * HD, width)
    qkv_grad = jnp.swapaxes(grad, 0, 1).astype(F32)[None]
    return mixed.reshape(latents.shape), latent_grad.reshape(latents.shape), qkv_grad


def across(distance):
    return [(2 * i + j, 2 * ((i + distance) % 32) + 1 - j) for i in range(32) for j in range(2)]


def solution(mesh):
    split = Mesh(mesh.devices.reshape(4, 4, 2, 8, 2), LON + HEAD)
    rows = P(None, HEAD, LON, None)
    return jax.shard_map(
        step,
        mesh=split,
        in_specs=(rows, rows, P(HEAD, None, None), P()),
        out_specs=(rows, rows, P(HEAD, None, None)),
        check_vma=False,
    )
```

```python
import jax
import jax.numpy as jnp
from jax import lax
from jax.experimental import pallas as pl
from jax.experimental.pallas import tpu as pltpu
from jax.sharding import Mesh, PartitionSpec as P

HD = 64
RANKS = 16
TOK = 72
HEAD = ("z", "yl")
LON = ("x", "yh", "core")
F32 = jnp.float32
BF16 = jnp.bfloat16


def dot_nt(a, b):
    return lax.dot_general(a, b, (((1,), (1,)), ((), ())), preferred_element_type=F32)


def dot_nn(a, b):
    return lax.dot_general(a, b, (((1,), (0,)), ((), ())), preferred_element_type=F32)


def dot_tn(a, b):
    return lax.dot_general(a, b, (((0,), (0,)), ((), ())), preferred_element_type=F32)


def call(body, outs, scratch=(), smem=(), n_in=1, flops=0, moved=0):
    specs = [
        pl.BlockSpec(memory_space=pltpu.SMEM if i in smem else pltpu.VMEM) for i in range(n_in)
    ]
    return pl.pallas_call(
        body,
        out_shape=[jax.ShapeDtypeStruct(s, d) for s, d in outs],
        in_specs=specs,
        out_specs=[pl.BlockSpec(memory_space=pltpu.VMEM) for _ in outs],
        scratch_shapes=list(scratch),
        cost_estimate=pl.CostEstimate(flops=flops, bytes_accessed=moved, transcendentals=0),
        compiler_params=pltpu.CompilerParams(vmem_limit_bytes=56 << 20),
    )


def low_half(shape):
    return lax.broadcasted_iota(jnp.int32, shape, len(shape) - 2) % 8 < 4


def pack_pair(value):
    half = value.shape[0] // 2
    groups = value.reshape(2, half * TOK // 8, 8, 128)
    first, second = groups[0], groups[1]
    low = low_half(first.shape)
    west = jnp.where(low, first, pltpu.roll(second, 4, 1))
    east = jnp.where(low, pltpu.roll(first, 4, 1), second)
    return west.reshape(half, TOK, 128), east.reshape(half, TOK, 128)


def unpack_pair(west, east):
    half = west.shape[0]
    west = west.reshape(half * TOK // 8, 8, 128)
    east = east.reshape(half * TOK // 8, 8, 128)
    low = low_half(west.shape)
    first = jnp.where(low, west, pltpu.roll(east, 4, 1))
    second = jnp.where(low, pltpu.roll(west, 4, 1), east)
    return first.reshape(half, TOK, 128), second.reshape(half, TOK, 128)


def fold_rows(value):
    rest = jnp.concatenate([value[40:], jnp.zeros((8, HD), F32)], axis=0)
    return jnp.concatenate([value[:40], rest], axis=1)


def unfold_rows(value):
    return jnp.concatenate([value[:, :HD], value[:32, HD:]], axis=0)


def turned(ref):
    return jnp.concatenate([ref[HD : 3 * HD], ref[0:HD]], axis=0)


def token_grad_kernel(grad_ref, weight_ref, out_ref):
    for pair in range(RANKS // 2):
        rows = weight_ref[2 * pair : 2 * pair + 2].reshape(2 * HD, -1)
        both = dot_nt(grad_ref[...], rows)
        out_ref[2 * pair] = fold_rows(both[:, :HD]).astype(BF16)
        out_ref[2 * pair + 1] = fold_rows(both[:, HD:]).astype(BF16)


def project_kernel(
    table_ref, tokens_ref, own_ref, other_ref,
    kv_ref, q_ref, swap_ref, far_ref, near_ref, far2_ref, near2_ref,
    kv32, kv32b,
):
    first_core = table_ref[8] == 0
    own, other = turned(own_ref), turned(other_ref)
    for chunk in range(2):
        rows = tokens_ref[chunk * 288 : (chunk + 1) * 288, :]
        proj = dot_nt(rows, own).astype(BF16).astype(F32)
        proj2 = dot_nt(rows, other).astype(BF16).astype(F32)
        for part in range(4):
            row = table_ref[chunk * 4 + part]
            piece = proj[part * TOK : (part + 1) * TOK]
            kv32[row] = piece[:, :128]
            kv_ref[row] = piece[:, :128].astype(BF16)
            q_ref[row] = piece[:, 128:].astype(BF16)
            piece = proj2[part * TOK : (part + 1) * TOK]
            kv32b[row] = piece[:, :128]
            swap_ref[row] = piece.astype(BF16)
    west, east = pack_pair(kv32[...])
    far_ref[...] = jnp.where(first_core, west, east).astype(BF16)
    near_ref[...] = jnp.where(first_core, east, west).astype(BF16)
    west, east = pack_pair(kv32b[...])
    far2_ref[...] = jnp.where(first_core, west, east).astype(BF16)
    near2_ref[...] = jnp.where(first_core, east, west).astype(BF16)


def attend_kernel(
    place_ref, kv_ref, q_ref, swapped_ref, grad_ref, far_ref, near_ref, far2_ref, near2_ref,
    out_ref, dq_ref, dkv_ref, to_far_ref, to_near_ref,
    keys, queries, halo, dhalo,
):
    scale = HD ** (-0.5)
    yl = place_ref[0]
    first_core = place_ref[1] == 0
    far, near = far_ref[...].astype(F32), near_ref[...].astype(F32)
    side = unpack_pair(jnp.where(first_core, near, far), jnp.where(first_core, far, near))
    far, near = far2_ref[...].astype(F32), near2_ref[...].astype(F32)
    side2 = unpack_pair(jnp.where(first_core, near, far), jnp.where(first_core, far, near))
    for row in range(8):
        mine, theirs = 2 * row + yl, 2 * row + 1 - yl
        keys[mine] = kv_ref[row].astype(F32)
        queries[mine] = q_ref[row].astype(F32)
        both = swapped_ref[row].astype(F32)
        keys[theirs] = both[:, :128]
        queries[theirs] = both[:, 128:]
        halo[mine] = side[row // 4][row % 4]
        halo[theirs] = side2[row // 4][row % 4]
    zeros = jnp.zeros((2 * TOK, HD), F32)
    windows = RANKS // 2
    for w in range(windows):
        lo, hi = max(2 * w - 1, 0), min(2 * w + 3, RANKS)
        count = (hi - lo) * TOK
        query = queries[2 * w : 2 * w + 2].reshape(2 * TOK, HD) * scale
        outer = jnp.concatenate(
            [unfold_rows(grad_ref[2 * w + i].astype(F32)) for i in range(2)], axis=0
        )
        lhs = jnp.concatenate(
            [
                jnp.concatenate([query, zeros], axis=1),
                jnp.concatenate([zeros, outer], axis=1),
            ],
            axis=0,
        ).astype(BF16)
        pairs = jnp.concatenate(
            [keys[lo:hi].reshape(count, 128), halo[lo:hi].reshape(count, 128)], axis=0
        ).astype(BF16)
        both = dot_nt(lhs, pairs)
        score, prob_grad = both[: 2 * TOK], both[2 * TOK :]
        powers = jnp.exp(score - jnp.max(score, axis=-1, keepdims=True))
        probs = powers * (1.0 / jnp.sum(powers, axis=-1, keepdims=True))
        centre = jnp.sum(probs * prob_grad, axis=-1, keepdims=True)
        score_grad = (probs * (prob_grad - centre)).astype(BF16)
        stack = jnp.concatenate([score_grad, probs.astype(BF16)], axis=0)
        mixed = dot_nn(stack, pairs)
        dq_ref[2 * w : 2 * w + 2] = (mixed[: 2 * TOK, :HD] * scale).reshape(2, TOK, HD)
        for i in range(2):
            rows = mixed[(2 + i) * TOK : (3 + i) * TOK, HD:]
            out_ref[2 * w + i] = fold_rows(rows).astype(BF16)
        grads = dot_tn(stack, lhs)
        own = grads[:count].reshape(hi - lo, TOK, 128)
        side = grads[count:].reshape(hi - lo, TOK, 128)
        for i, rank in enumerate(range(lo, hi)):
            seen = w > 0 and rank <= 2 * w
            if seen:
                dkv_ref[rank] += own[i]
                dhalo[rank] += side[i]
            else:
                dkv_ref[rank] = own[i]
                dhalo[rank] = side[i]
    to_e, to_w = pack_pair(dhalo[...])
    to_far_ref[...] = jnp.where(first_core, to_w, to_e).astype(BF16)
    to_near_ref[...] = jnp.where(first_core, to_e, to_w).astype(BF16)


def combine_kernel(
    place_ref, dq_ref, dkv_ref, far_ref, near_ref, pg_ref, mine_ref, swap_ref, pg32
):
    yl = place_ref[0]
    first_core = place_ref[1] == 0
    far, near = far_ref[...].astype(F32), near_ref[...].astype(F32)
    first, second = unpack_pair(jnp.where(first_core, far, near), jnp.where(first_core, near, far))
    for half, add in ((0, first), (1, second)):
        span = slice(8 * half, 8 * half + 8)
        pg32[span, :, 0:128] = dkv_ref[span] + add
        pg32[span, :, 128:192] = dq_ref[span]
    pg_ref[...] = pg32[...].astype(BF16)
    for row in range(8):
        mine_ref[row] = pg32[2 * row + yl].astype(BF16)
        swap_ref[row] = pg32[2 * row + 1 - yl].astype(BF16)


def share_kernel(table_ref, mine_ref, got_ref, own_ref, other_ref, *out_refs):
    own, other = turned(own_ref), turned(other_ref)
    for chunk in range(2):
        picks = [table_ref[4 * chunk + i] for i in range(4)]
        rows = jnp.concatenate([mine_ref[p].astype(F32) for p in picks], axis=0).astype(BF16)
        rows2 = jnp.concatenate([got_ref[p].astype(F32) for p in picks], axis=0).astype(BF16)
        part = dot_nn(rows, own) + dot_nn(rows2, other)
        for i in range(4):
            out_refs[4 * chunk + i][...] = part[i * TOK : (i + 1) * TOK].astype(BF16)


def weight_grad_kernel(table_ref, tokens_ref, tokens2_ref, pg_ref, piece_ref):
    total = None
    for chunk in range(4):
        rows = jnp.concatenate(
            [pg_ref[table_ref[4 * chunk + i]].astype(F32) for i in range(4)], axis=0
        ).astype(BF16)
        source = tokens_ref if chunk < 2 else tokens2_ref
        span = slice((chunk % 2) * 288, (chunk % 2) * 288 + 288)
        part = dot_tn(rows, source[span, :])
        total = part if total is None else total + part
    total = jnp.concatenate([total[128:192], total[0:128]], axis=0).astype(BF16)
    for g in range(4):
        for j in range(8):
            piece_ref[8 * g + j] = total[48 * g : 48 * g + 48, 128 * j : 128 * j + 128]


def mix_kernel(att_ref, weight_ref, out_ref):
    rows = [unfold_rows(att_ref[h].astype(F32)) for h in range(RANKS)]
    rows = jnp.concatenate(rows, axis=1).astype(BF16)
    out_ref[...] = dot_nn(rows, weight_ref[...]).astype(BF16)


def shift(value, axis, size, distance):
    return lax.ppermute(value, axis, [(i, (i + distance) % size) for i in range(size)])


def exchange(value, axis):
    return lax.all_to_all(value, axis, 0, 0, tiled=True)


def step(latents, out_grad, qkv_weight, out_weight):
    width = latents.shape[-1]
    z, yl, core = (lax.axis_index(a).astype(jnp.int32) for a in ("z", "yl", "core"))
    mine = latents.reshape(TOK, width)
    own = jnp.swapaxes(qkv_weight[0], 0, 1)
    d1, d7, d2, d6 = (shift(mine, "z", 8, d) for d in (1, 7, 2, 6))
    other = shift(own, "yl", 2, 1)
    d3, d5 = shift(d2, "z", 8, 1), shift(d6, "z", 8, -1)
    d4 = shift(d2, "z", 8, 2)
    close = jnp.concatenate([mine, d1, d7, d2, d6], axis=0)
    close2 = shift(close, "yl", 2, 1)
    distant = jnp.concatenate([d3, d5, d4], axis=0)
    distant2 = shift(distant, "yl", 2, 1)
    tokens = jnp.concatenate([close, distant], axis=0)
    tokens2 = jnp.concatenate([close2, distant2], axis=0)
    distance = jnp.array([0, 1, 7, 2, 6, 3, 5, 4], jnp.int32)
    rows = ((z - distance) % 8).astype(jnp.int32)
    place = jnp.stack([yl, core])

    (token_grad,) = call(
        token_grad_kernel, [((RANKS, 40, 128), BF16)], n_in=2, flops=2 * TOK * width * width
    )(out_grad.reshape(TOK, width), out_weight)
    band_grad = exchange(token_grad, HEAD)

    kv, query, swap, far, near, far2, near2 = call(
        project_kernel,
        [((8, TOK, 128), BF16), ((8, TOK, HD), BF16), ((8, TOK, 3 * HD), BF16)]
        + [((4, TOK, 128), BF16)] * 4,
        scratch=[pltpu.VMEM((8, TOK, 128), F32)] * 2,
        smem=(0,),
        n_in=4,
        flops=2 * 1152 * 192 * width,
    )(jnp.concatenate([rows, core.reshape(1)]), tokens, own, other)
    far, near = send_far(far), shift(near, "core", 2, 1)
    far2, near2 = send_far(far2, 1), send_near(near2, 1)
    swapped = shift(swap, "yl", 2, 1)
    attended, dq, dkv, grad_far, grad_near = call(
        attend_kernel,
        [
            ((RANKS, 40, 128), BF16),
            ((RANKS, TOK, HD), F32),
            ((RANKS, TOK, 128), F32),
            ((8, TOK, 128), BF16),
            ((8, TOK, 128), BF16),
        ],
        scratch=[
            pltpu.VMEM((RANKS, TOK, 128), F32),
            pltpu.VMEM((RANKS, TOK, HD), F32),
            pltpu.VMEM((RANKS, TOK, 128), F32),
            pltpu.VMEM((RANKS, TOK, 128), F32),
        ],
        smem=(0,),
        n_in=9,
        flops=8 * 6 * 2 * 144 * 576 * 128,
    )(place, kv, query, swapped, band_grad, far, near, far2, near2)
    grad_far, grad_near = send_far(grad_far), shift(grad_near, "core", 2, 1)
    token_att = exchange(attended, HEAD)

    pg, pg_mine, pg_swap = call(
        combine_kernel,
        [((RANKS, TOK, 3 * HD), BF16), ((8, TOK, 3 * HD), BF16), ((8, TOK, 3 * HD), BF16)],
        scratch=[pltpu.VMEM((RANKS, TOK, 3 * HD), F32)],
        smem=(0,),
        n_in=5,
        flops=1 << 20,
    )(place, dq, dkv, grad_far, grad_near)
    pg_got = shift(pg_swap, "yl", 2, 1)
    (pieces,) = call(
        weight_grad_kernel,
        [((32, 48, 128), BF16)],
        smem=(0,),
        n_in=4,
        flops=2 * 1152 * 192 * width,
    )(
        jnp.concatenate([2 * rows + yl, 2 * rows + 1 - yl]).astype(jnp.int32),
        tokens, tokens2, pg,
    )
    pieces = exchange(pieces, LON)
    reach = (4, 3, 5, 2, 6, 1, 7, 0)
    shares = call(
        share_kernel,
        [((TOK, width), BF16)] * 8,
        smem=(0,),
        n_in=5,
        flops=2 * 576 * 384 * width,
    )(((z + jnp.array(reach, jnp.int32)) % 8).astype(jnp.int32), pg_mine, pg_got, own, other)
    passed = shift(shares[0], "z", 8, -1)
    shares = list(shares[1:])
    shares[1] = (shares[1].astype(F32) + passed.astype(F32)).astype(BF16)
    shares = [shift(s, "z", 8, d) if d else s for s, d in zip(shares, reach[1:])]
    summed = jnp.sum(pieces.astype(F32), axis=0).astype(BF16)
    copies = exchange(jnp.broadcast_to(summed[None], (32, 48, 128)), LON)
    (mixed,) = call(mix_kernel, [((TOK, width), BF16)], n_in=2, flops=2 * TOK * width * width)(
        token_att, out_weight.reshape(width, width)
    )
    latent_grad = sum(s.astype(F32) for s in shares).astype(BF16)
    grad = copies.reshape(4, 8, 48, 128).transpose(0, 2, 1, 3).reshape(3 * HD, width)
    qkv_grad = jnp.swapaxes(grad, 0, 1).astype(F32)[None]
    return mixed.reshape(latents.shape), latent_grad.reshape(latents.shape), qkv_grad


def send_far(value, turn=0):
    routes = [
        (2 * i + j, 2 * ((i + (1 if i % 2 else -1)) % 32) + (j ^ turn))
        for i in range(32)
        for j in range(2)
    ]
    return lax.ppermute(value, LON + ("yl",), routes)


def send_near(value, turn=0):
    routes = [(2 * i + j, 2 * (i ^ 1) + (j ^ turn)) for i in range(32) for j in range(2)]
    return lax.ppermute(value, LON + ("yl",), routes)


def solution(mesh):
    split = Mesh(mesh.devices.reshape(4, 4, 2, 8, 2), LON + HEAD)
    rows = P(None, HEAD, LON, None)
    return jax.shard_map(
        step,
        mesh=split,
        in_specs=(rows, rows, P(HEAD, None, None), P()),
        out_specs=(rows, rows, P(HEAD, None, None)),
        check_vma=False,
    )
```

```python
import jax
import jax.numpy as jnp
from jax import lax
from jax.experimental import pallas as pl
from jax.experimental.pallas import tpu as pltpu
from jax.sharding import Mesh, PartitionSpec as P

HD = 64
RANKS = 16
TOK = 72
HEAD = ("z", "yl")
LON = ("x", "yh", "core")
F32 = jnp.float32
BF16 = jnp.bfloat16


def dot_nt(a, b):
    return lax.dot_general(a, b, (((1,), (1,)), ((), ())), preferred_element_type=F32)


def dot_nn(a, b):
    return lax.dot_general(a, b, (((1,), (0,)), ((), ())), preferred_element_type=F32)


def dot_tn(a, b):
    return lax.dot_general(a, b, (((0,), (0,)), ((), ())), preferred_element_type=F32)


def call(body, outs, scratch=(), smem=(), n_in=1, flops=0, moved=0):
    specs = [
        pl.BlockSpec(memory_space=pltpu.SMEM if i in smem else pltpu.VMEM) for i in range(n_in)
    ]
    return pl.pallas_call(
        body,
        out_shape=[jax.ShapeDtypeStruct(s, d) for s, d in outs],
        in_specs=specs,
        out_specs=[pl.BlockSpec(memory_space=pltpu.VMEM) for _ in outs],
        scratch_shapes=list(scratch),
        cost_estimate=pl.CostEstimate(flops=flops, bytes_accessed=moved, transcendentals=0),
        compiler_params=pltpu.CompilerParams(vmem_limit_bytes=56 << 20),
    )


def low_half(shape):
    return lax.broadcasted_iota(jnp.int32, shape, len(shape) - 2) % 8 < 4


def pack_pair(value):
    half = value.shape[0] // 2
    groups = value.reshape(2, half * TOK // 8, 8, 128)
    first, second = groups[0], groups[1]
    low = low_half(first.shape)
    west = jnp.where(low, first, pltpu.roll(second, 4, 1))
    east = jnp.where(low, pltpu.roll(first, 4, 1), second)
    return west.reshape(half, TOK, 128), east.reshape(half, TOK, 128)


def unpack_pair(west, east):
    half = west.shape[0]
    west = west.reshape(half * TOK // 8, 8, 128)
    east = east.reshape(half * TOK // 8, 8, 128)
    low = low_half(west.shape)
    first = jnp.where(low, west, pltpu.roll(east, 4, 1))
    second = jnp.where(low, pltpu.roll(west, 4, 1), east)
    return first.reshape(half, TOK, 128), second.reshape(half, TOK, 128)


def fold_rows(value):
    rest = jnp.concatenate([value[40:], jnp.zeros((8, HD), F32)], axis=0)
    return jnp.concatenate([value[:40], rest], axis=1)


def unfold_rows(value):
    return jnp.concatenate([value[:, :HD], value[:32, HD:]], axis=0)


def turned(ref):
    return jnp.concatenate([ref[HD : 3 * HD], ref[0:HD]], axis=0)


def token_grad_kernel(grad_ref, weight_ref, out_ref):
    for pair in range(RANKS // 2):
        rows = weight_ref[2 * pair : 2 * pair + 2].reshape(2 * HD, -1)
        both = dot_nt(grad_ref[...], rows)
        out_ref[2 * pair] = fold_rows(both[:, :HD]).astype(BF16)
        out_ref[2 * pair + 1] = fold_rows(both[:, HD:]).astype(BF16)


def project_kernel(
    table_ref, tokens_ref, own_ref, other_ref,
    kv_ref, q_ref, swap_ref, far_ref, near_ref, far2_ref, near2_ref,
    kv32, kv32b,
):
    first_core = table_ref[8] == 0
    own, other = turned(own_ref), turned(other_ref)
    for chunk in range(2):
        rows = tokens_ref[chunk * 288 : (chunk + 1) * 288, :]
        proj = dot_nt(rows, own).astype(BF16).astype(F32)
        proj2 = dot_nt(rows, other).astype(BF16).astype(F32)
        for part in range(4):
            row = table_ref[chunk * 4 + part]
            piece = proj[part * TOK : (part + 1) * TOK]
            kv32[row] = piece[:, :128]
            kv_ref[row] = piece[:, :128].astype(BF16)
            q_ref[row] = piece[:, 128:].astype(BF16)
            piece = proj2[part * TOK : (part + 1) * TOK]
            kv32b[row] = piece[:, :128]
            swap_ref[row] = piece.astype(BF16)
    west, east = pack_pair(kv32[...])
    far_ref[...] = jnp.where(first_core, west, east).astype(BF16)
    near_ref[...] = jnp.where(first_core, east, west).astype(BF16)
    west, east = pack_pair(kv32b[...])
    far2_ref[...] = jnp.where(first_core, west, east).astype(BF16)
    near2_ref[...] = jnp.where(first_core, east, west).astype(BF16)


def attend_kernel(
    place_ref, kv_ref, q_ref, swapped_ref, grad_ref, far_ref, near_ref, far2_ref, near2_ref,
    out_ref, dq_ref, dkv_ref, to_far_ref, to_near_ref,
    keys, queries, halo, dhalo,
):
    scale = HD ** (-0.5)
    yl = place_ref[0]
    first_core = place_ref[1] == 0
    far, near = far_ref[...].astype(F32), near_ref[...].astype(F32)
    side = unpack_pair(jnp.where(first_core, near, far), jnp.where(first_core, far, near))
    far, near = far2_ref[...].astype(F32), near2_ref[...].astype(F32)
    side2 = unpack_pair(jnp.where(first_core, near, far), jnp.where(first_core, far, near))
    for row in range(8):
        mine, theirs = 2 * row + yl, 2 * row + 1 - yl
        keys[mine] = kv_ref[row].astype(F32)
        queries[mine] = q_ref[row].astype(F32)
        both = swapped_ref[row].astype(F32)
        keys[theirs] = both[:, :128]
        queries[theirs] = both[:, 128:]
        halo[mine] = side[row // 4][row % 4]
        halo[theirs] = side2[row // 4][row % 4]
    zeros = jnp.zeros((2 * TOK, HD), F32)
    windows = RANKS // 2
    for w in range(windows):
        lo, hi = max(2 * w - 1, 0), min(2 * w + 3, RANKS)
        count = (hi - lo) * TOK
        query = queries[2 * w : 2 * w + 2].reshape(2 * TOK, HD) * scale
        outer = jnp.concatenate(
            [unfold_rows(grad_ref[2 * w + i].astype(F32)) for i in range(2)], axis=0
        )
        lhs = jnp.concatenate(
            [
                jnp.concatenate([query, zeros], axis=1),
                jnp.concatenate([zeros, outer], axis=1),
            ],
            axis=0,
        ).astype(BF16)
        pairs = jnp.concatenate(
            [keys[lo:hi].reshape(count, 128), halo[lo:hi].reshape(count, 128)], axis=0
        ).astype(BF16)
        both = dot_nt(lhs, pairs)
        score, prob_grad = both[: 2 * TOK], both[2 * TOK :]
        powers = jnp.exp(score - jnp.max(score, axis=-1, keepdims=True))
        probs = powers * (1.0 / jnp.sum(powers, axis=-1, keepdims=True))
        centre = jnp.sum(probs * prob_grad, axis=-1, keepdims=True)
        score_grad = (probs * (prob_grad - centre)).astype(BF16)
        stack = jnp.concatenate([score_grad, probs.astype(BF16)], axis=0)
        mixed = dot_nn(stack, pairs)
        dq_ref[2 * w : 2 * w + 2] = (mixed[: 2 * TOK, :HD] * scale).reshape(2, TOK, HD)
        for i in range(2):
            rows = mixed[(2 + i) * TOK : (3 + i) * TOK, HD:]
            out_ref[2 * w + i] = fold_rows(rows).astype(BF16)
        grads = dot_tn(stack, lhs)
        own = grads[:count].reshape(hi - lo, TOK, 128)
        side = grads[count:].reshape(hi - lo, TOK, 128)
        for i, rank in enumerate(range(lo, hi)):
            seen = w > 0 and rank <= 2 * w
            if seen:
                dkv_ref[rank] += own[i]
                dhalo[rank] += side[i]
            else:
                dkv_ref[rank] = own[i]
                dhalo[rank] = side[i]
    to_e, to_w = pack_pair(dhalo[...])
    to_far_ref[...] = jnp.where(first_core, to_w, to_e).astype(BF16)
    to_near_ref[...] = jnp.where(first_core, to_e, to_w).astype(BF16)


def combine_kernel(
    place_ref, dq_ref, dkv_ref, far_ref, near_ref, pg_ref, mine_ref, swap_ref, pg32
):
    yl = place_ref[0]
    first_core = place_ref[1] == 0
    far, near = far_ref[...].astype(F32), near_ref[...].astype(F32)
    first, second = unpack_pair(jnp.where(first_core, far, near), jnp.where(first_core, near, far))
    for half, add in ((0, first), (1, second)):
        span = slice(8 * half, 8 * half + 8)
        pg32[span, :, 0:128] = dkv_ref[span] + add
        pg32[span, :, 128:192] = dq_ref[span]
    pg_ref[...] = pg32[...].astype(BF16)
    for row in range(8):
        mine_ref[row] = pg32[2 * row + yl].astype(BF16)
        swap_ref[row] = pg32[2 * row + 1 - yl].astype(BF16)


def share_kernel(table_ref, mine_ref, got_ref, own_ref, other_ref, *out_refs):
    own, other = turned(own_ref), turned(other_ref)
    for chunk in range(2):
        picks = [table_ref[4 * chunk + i] for i in range(4)]
        rows = jnp.concatenate([mine_ref[p].astype(F32) for p in picks], axis=0).astype(BF16)
        rows2 = jnp.concatenate([got_ref[p].astype(F32) for p in picks], axis=0).astype(BF16)
        part = dot_nn(rows, own) + dot_nn(rows2, other)
        for i in range(4):
            out_refs[4 * chunk + i][...] = part[i * TOK : (i + 1) * TOK].astype(BF16)


def weight_grad_kernel(table_ref, tokens_ref, tokens2_ref, pg_ref, piece_ref):
    total = None
    for chunk in range(4):
        rows = jnp.concatenate(
            [pg_ref[table_ref[4 * chunk + i]].astype(F32) for i in range(4)], axis=0
        ).astype(BF16)
        source = tokens_ref if chunk < 2 else tokens2_ref
        span = slice((chunk % 2) * 288, (chunk % 2) * 288 + 288)
        part = dot_tn(rows, source[span, :])
        total = part if total is None else total + part
    total = jnp.concatenate([total[128:192], total[0:128]], axis=0).astype(BF16)
    for g in range(4):
        for j in range(8):
            piece_ref[8 * g + j] = total[48 * g : 48 * g + 48, 128 * j : 128 * j + 128]


def mix_kernel(att_ref, weight_ref, out_ref):
    rows = [unfold_rows(att_ref[h].astype(F32)) for h in range(RANKS)]
    rows = jnp.concatenate(rows, axis=1).astype(BF16)
    out_ref[...] = dot_nn(rows, weight_ref[...]).astype(BF16)


def shift(value, axis, size, distance):
    return lax.ppermute(value, axis, [(i, (i + distance) % size) for i in range(size)])


def exchange(value, axis):
    return lax.all_to_all(value, axis, 0, 0, tiled=True)


def step(latents, out_grad, qkv_weight, out_weight):
    width = latents.shape[-1]
    z, yl, core = (lax.axis_index(a).astype(jnp.int32) for a in ("z", "yl", "core"))
    mine = latents.reshape(TOK, width)
    own = jnp.swapaxes(qkv_weight[0], 0, 1)
    d1, d7, d2, d6 = (shift(mine, "z", 8, d) for d in (1, 7, 2, 6))
    other = shift(own, "yl", 2, 1)
    d3, d5 = shift(d2, "z", 8, 1), shift(d6, "z", 8, -1)
    d4 = shift(d2, "z", 8, 2)
    tokens = jnp.concatenate([mine, d1, d7, d2, d6, d3, d5, d4], axis=0)
    tokens2 = shift(tokens, "yl", 2, 1)
    distance = jnp.array([0, 1, 7, 2, 6, 3, 5, 4], jnp.int32)
    rows = ((z - distance) % 8).astype(jnp.int32)
    place = jnp.stack([yl, core])

    (token_grad,) = call(
        token_grad_kernel, [((RANKS, 40, 128), BF16)], n_in=2, flops=2 * TOK * width * width
    )(out_grad.reshape(TOK, width), out_weight)
    band_grad = exchange(token_grad, HEAD)

    kv, query, swap, far, near, far2, near2 = call(
        project_kernel,
        [((8, TOK, 128), BF16), ((8, TOK, HD), BF16), ((8, TOK, 3 * HD), BF16)]
        + [((4, TOK, 128), BF16)] * 4,
        scratch=[pltpu.VMEM((8, TOK, 128), F32)] * 2,
        smem=(0,),
        n_in=4,
        flops=2 * 1152 * 192 * width,
    )(jnp.concatenate([rows, core.reshape(1)]), tokens, own, other)
    far, near = send_far(far), shift(near, "core", 2, 1)
    far2, near2 = send_far(far2, 1), send_near(near2, 1)
    swapped = shift(swap, "yl", 2, 1)
    attended, dq, dkv, grad_far, grad_near = call(
        attend_kernel,
        [
            ((RANKS, 40, 128), BF16),
            ((RANKS, TOK, HD), F32),
            ((RANKS, TOK, 128), F32),
            ((8, TOK, 128), BF16),
            ((8, TOK, 128), BF16),
        ],
        scratch=[
            pltpu.VMEM((RANKS, TOK, 128), F32),
            pltpu.VMEM((RANKS, TOK, HD), F32),
            pltpu.VMEM((RANKS, TOK, 128), F32),
            pltpu.VMEM((RANKS, TOK, 128), F32),
        ],
        smem=(0,),
        n_in=9,
        flops=8 * 6 * 2 * 144 * 576 * 128,
    )(place, kv, query, swapped, band_grad, far, near, far2, near2)
    grad_far, grad_near = send_far(grad_far), shift(grad_near, "core", 2, 1)
    token_att = exchange(attended, HEAD)

    pg, pg_mine, pg_swap = call(
        combine_kernel,
        [((RANKS, TOK, 3 * HD), BF16), ((8, TOK, 3 * HD), BF16), ((8, TOK, 3 * HD), BF16)],
        scratch=[pltpu.VMEM((RANKS, TOK, 3 * HD), F32)],
        smem=(0,),
        n_in=5,
        flops=1 << 20,
    )(place, dq, dkv, grad_far, grad_near)
    pg_got = shift(pg_swap, "yl", 2, 1)
    (pieces,) = call(
        weight_grad_kernel,
        [((32, 48, 128), BF16)],
        smem=(0,),
        n_in=4,
        flops=2 * 1152 * 192 * width,
    )(
        jnp.concatenate([2 * rows + yl, 2 * rows + 1 - yl]).astype(jnp.int32),
        tokens, tokens2, pg,
    )
    pieces = exchange(pieces, LON)
    reach = (4, 3, 5, 2, 6, 1, 7, 0)
    shares = call(
        share_kernel,
        [((TOK, width), BF16)] * 8,
        smem=(0,),
        n_in=5,
        flops=2 * 576 * 384 * width,
    )(((z + jnp.array(reach, jnp.int32)) % 8).astype(jnp.int32), pg_mine, pg_got, own, other)
    passed = shift(shares[0], "z", 8, -1)
    shares = list(shares[1:])
    shares[1] = (shares[1].astype(F32) + passed.astype(F32)).astype(BF16)
    shares = [shift(s, "z", 8, d) if d else s for s, d in zip(shares, reach[1:])]
    summed = jnp.sum(pieces.astype(F32), axis=0).astype(BF16)
    copies = exchange(jnp.broadcast_to(summed[None], (32, 48, 128)), LON)
    (mixed,) = call(mix_kernel, [((TOK, width), BF16)], n_in=2, flops=2 * TOK * width * width)(
        token_att, out_weight.reshape(width, width)
    )
    latent_grad = sum(s.astype(F32) for s in shares).astype(BF16)
    grad = copies.reshape(4, 8, 48, 128).transpose(0, 2, 1, 3).reshape(3 * HD, width)
    qkv_grad = jnp.swapaxes(grad, 0, 1).astype(F32)[None]
    return mixed.reshape(latents.shape), latent_grad.reshape(latents.shape), qkv_grad


def send_far(value, turn=0):
    routes = [
        (2 * i + j, 2 * ((i + (1 if i % 2 else -1)) % 32) + (j ^ turn))
        for i in range(32)
        for j in range(2)
    ]
    return lax.ppermute(value, LON + ("yl",), routes)


def send_near(value, turn=0):
    routes = [(2 * i + j, 2 * (i ^ 1) + (j ^ turn)) for i in range(32) for j in range(2)]
    return lax.ppermute(value, LON + ("yl",), routes)


def solution(mesh):
    split = Mesh(mesh.devices.reshape(4, 4, 2, 8, 2), LON + HEAD)
    rows = P(None, HEAD, LON, None)
    return jax.shard_map(
        step,
        mesh=split,
        in_specs=(rows, rows, P(HEAD, None, None), P()),
        out_specs=(rows, rows, P(HEAD, None, None)),
        check_vma=False,
    )
```

```python
import jax
import jax.numpy as jnp
from jax import lax
from jax.experimental import pallas as pl
from jax.experimental.pallas import tpu as pltpu
from jax.sharding import Mesh, PartitionSpec as P

HD = 64
RANKS = 16
TOK = 72
HEAD = ("z", "yl")
LON = ("x", "yh", "core")
F32 = jnp.float32
BF16 = jnp.bfloat16


def dot_nt(a, b):
    return lax.dot_general(a, b, (((1,), (1,)), ((), ())), preferred_element_type=F32)


def dot_nn(a, b):
    return lax.dot_general(a, b, (((1,), (0,)), ((), ())), preferred_element_type=F32)


def dot_tn(a, b):
    return lax.dot_general(a, b, (((0,), (0,)), ((), ())), preferred_element_type=F32)


def call(body, outs, scratch=(), smem=(), n_in=1, flops=0, moved=0):
    specs = [
        pl.BlockSpec(memory_space=pltpu.SMEM if i in smem else pltpu.VMEM) for i in range(n_in)
    ]
    return pl.pallas_call(
        body,
        out_shape=[jax.ShapeDtypeStruct(s, d) for s, d in outs],
        in_specs=specs,
        out_specs=[pl.BlockSpec(memory_space=pltpu.VMEM) for _ in outs],
        scratch_shapes=list(scratch),
        cost_estimate=pl.CostEstimate(flops=flops, bytes_accessed=moved, transcendentals=0),
        compiler_params=pltpu.CompilerParams(vmem_limit_bytes=56 << 20),
    )


def low_half(shape):
    return lax.broadcasted_iota(jnp.int32, shape, len(shape) - 2) % 8 < 4


def pack_pair(value):
    half = value.shape[0] // 2
    groups = value.reshape(2, half * TOK // 8, 8, 128)
    first, second = groups[0], groups[1]
    low = low_half(first.shape)
    west = jnp.where(low, first, pltpu.roll(second, 4, 1))
    east = jnp.where(low, pltpu.roll(first, 4, 1), second)
    return west.reshape(half, TOK, 128), east.reshape(half, TOK, 128)


def unpack_pair(west, east):
    half = west.shape[0]
    west = west.reshape(half * TOK // 8, 8, 128)
    east = east.reshape(half * TOK // 8, 8, 128)
    low = low_half(west.shape)
    first = jnp.where(low, west, pltpu.roll(east, 4, 1))
    second = jnp.where(low, pltpu.roll(west, 4, 1), east)
    return first.reshape(half, TOK, 128), second.reshape(half, TOK, 128)


def fold_rows(value):
    rest = jnp.concatenate([value[40:], jnp.zeros((8, HD), F32)], axis=0)
    return jnp.concatenate([value[:40], rest], axis=1)


def unfold_rows(value):
    return jnp.concatenate([value[:, :HD], value[:32, HD:]], axis=0)


def turned(ref):
    return jnp.concatenate([ref[HD : 3 * HD], ref[0:HD]], axis=0)


def token_grad_kernel(grad_ref, weight_ref, out_ref):
    for pair in range(RANKS // 2):
        rows = weight_ref[2 * pair : 2 * pair + 2].reshape(2 * HD, -1)
        both = dot_nt(grad_ref[...], rows)
        out_ref[2 * pair] = fold_rows(both[:, :HD]).astype(BF16)
        out_ref[2 * pair + 1] = fold_rows(both[:, HD:]).astype(BF16)


def project_kernel(
    table_ref, t0_ref, t1_ref, t2_ref, t3_ref, own_ref, other_ref,
    kv_ref, q_ref, swap_ref, far_ref, near_ref, far2_ref, near2_ref,
    kv32, kv32b,
):
    first_core = table_ref[8] == 0
    own, other = turned(own_ref), turned(other_ref)
    for chunk, (a_ref, b_ref) in enumerate(((t0_ref, t1_ref), (t2_ref, t3_ref))):
        rows = jnp.concatenate([a_ref[...], b_ref[...]], axis=0)
        proj = dot_nt(rows, own).astype(BF16).astype(F32)
        proj2 = dot_nt(rows, other).astype(BF16).astype(F32)
        for part in range(4):
            row = table_ref[chunk * 4 + part]
            piece = proj[part * TOK : (part + 1) * TOK]
            kv32[row] = piece[:, :128]
            kv_ref[row] = piece[:, :128].astype(BF16)
            q_ref[row] = piece[:, 128:].astype(BF16)
            piece = proj2[part * TOK : (part + 1) * TOK]
            kv32b[row] = piece[:, :128]
            swap_ref[row] = piece.astype(BF16)
    west, east = pack_pair(kv32[...])
    far_ref[...] = jnp.where(first_core, west, east).astype(BF16)
    near_ref[...] = jnp.where(first_core, east, west).astype(BF16)
    west, east = pack_pair(kv32b[...])
    far2_ref[...] = jnp.where(first_core, west, east).astype(BF16)
    near2_ref[...] = jnp.where(first_core, east, west).astype(BF16)


def attend_kernel(
    place_ref, kv_ref, q_ref, swapped_ref, grad_ref, far_ref, near_ref, far2_ref, near2_ref,
    out_ref, dq_ref, dkv_ref, to_far_ref, to_near_ref,
    keys, queries, halo, dhalo,
):
    scale = HD ** (-0.5)
    yl = place_ref[0]
    first_core = place_ref[1] == 0
    far, near = far_ref[...].astype(F32), near_ref[...].astype(F32)
    side = unpack_pair(jnp.where(first_core, near, far), jnp.where(first_core, far, near))
    far, near = far2_ref[...].astype(F32), near2_ref[...].astype(F32)
    side2 = unpack_pair(jnp.where(first_core, near, far), jnp.where(first_core, far, near))
    for row in range(8):
        mine, theirs = 2 * row + yl, 2 * row + 1 - yl
        keys[mine] = kv_ref[row].astype(F32)
        queries[mine] = q_ref[row].astype(F32)
        both = swapped_ref[row].astype(F32)
        keys[theirs] = both[:, :128]
        queries[theirs] = both[:, 128:]
        halo[mine] = side[row // 4][row % 4]
        halo[theirs] = side2[row // 4][row % 4]
    zeros = jnp.zeros((2 * TOK, HD), F32)
    windows = RANKS // 2
    for w in range(windows):
        lo, hi = max(2 * w - 1, 0), min(2 * w + 3, RANKS)
        count = (hi - lo) * TOK
        query = queries[2 * w : 2 * w + 2].reshape(2 * TOK, HD) * scale
        outer = jnp.concatenate(
            [unfold_rows(grad_ref[2 * w + i].astype(F32)) for i in range(2)], axis=0
        )
        lhs = jnp.concatenate(
            [
                jnp.concatenate([query, zeros], axis=1),
                jnp.concatenate([zeros, outer], axis=1),
            ],
            axis=0,
        ).astype(BF16)
        pairs = jnp.concatenate(
            [keys[lo:hi].reshape(count, 128), halo[lo:hi].reshape(count, 128)], axis=0
        ).astype(BF16)
        both = dot_nt(lhs, pairs)
        score, prob_grad = both[: 2 * TOK], both[2 * TOK :]
        powers = jnp.exp(score - jnp.max(score, axis=-1, keepdims=True))
        probs = powers * (1.0 / jnp.sum(powers, axis=-1, keepdims=True))
        centre = jnp.sum(probs * prob_grad, axis=-1, keepdims=True)
        score_grad = (probs * (prob_grad - centre)).astype(BF16)
        stack = jnp.concatenate([score_grad, probs.astype(BF16)], axis=0)
        mixed = dot_nn(stack, pairs)
        dq_ref[2 * w : 2 * w + 2] = (mixed[: 2 * TOK, :HD] * scale).reshape(2, TOK, HD)
        for i in range(2):
            rows = mixed[(2 + i) * TOK : (3 + i) * TOK, HD:]
            out_ref[2 * w + i] = fold_rows(rows).astype(BF16)
        grads = dot_tn(stack, lhs)
        own = grads[:count].reshape(hi - lo, TOK, 128)
        side = grads[count:].reshape(hi - lo, TOK, 128)
        for i, rank in enumerate(range(lo, hi)):
            seen = w > 0 and rank <= 2 * w
            if seen:
                dkv_ref[rank] += own[i]
                dhalo[rank] += side[i]
            else:
                dkv_ref[rank] = own[i]
                dhalo[rank] = side[i]
    to_e, to_w = pack_pair(dhalo[...])
    to_far_ref[...] = jnp.where(first_core, to_w, to_e).astype(BF16)
    to_near_ref[...] = jnp.where(first_core, to_e, to_w).astype(BF16)


def combine_kernel(
    place_ref, dq_ref, dkv_ref, far_ref, near_ref, mine_ref, swap_ref, pg32
):
    yl = place_ref[0]
    first_core = place_ref[1] == 0
    far, near = far_ref[...].astype(F32), near_ref[...].astype(F32)
    first, second = unpack_pair(jnp.where(first_core, far, near), jnp.where(first_core, near, far))
    for half, add in ((0, first), (1, second)):
        span = slice(8 * half, 8 * half + 8)
        pg32[span, :, 0:128] = dkv_ref[span] + add
        pg32[span, :, 128:192] = dq_ref[span]
    for row in range(8):
        mine_ref[row] = pg32[2 * row + yl].astype(BF16)
        swap_ref[row] = pg32[2 * row + 1 - yl].astype(BF16)


def share_kernel(table_ref, mine_ref, got_ref, own_ref, other_ref, *out_refs):
    own, other = turned(own_ref), turned(other_ref)
    for chunk in range(2):
        picks = [table_ref[4 * chunk + i] for i in range(4)]
        rows = jnp.concatenate([mine_ref[p].astype(F32) for p in picks], axis=0).astype(BF16)
        rows2 = jnp.concatenate([got_ref[p].astype(F32) for p in picks], axis=0).astype(BF16)
        part = (dot_nn(rows, own) + dot_nn(rows2, other)).astype(BF16)
        if chunk == 0:
            out_refs[0][...] = part[: 2 * TOK]
            out_refs[1][...] = part[2 * TOK :]
        else:
            for i in range(4):
                out_refs[2 + i][...] = part[i * TOK : (i + 1) * TOK]


def weight_grad_kernel(table_ref, pg_ref, t0_ref, t1_ref, t2_ref, t3_ref, out_ref):
    total = None
    for chunk, (a_ref, b_ref) in enumerate(((t0_ref, t1_ref), (t2_ref, t3_ref))):
        rows = jnp.concatenate(
            [pg_ref[table_ref[4 * chunk + i]].astype(F32) for i in range(4)], axis=0
        ).astype(BF16)
        part = dot_tn(rows, jnp.concatenate([a_ref[...], b_ref[...]], axis=0))
        total = part if total is None else total + part
    out_ref[...] = total.astype(out_ref.dtype)


def piece_kernel(own_ref, got_ref, piece_ref):
    for g in range(4):
        for start in range(48 * g, 48 * g + 48, 16):
            row = (start + 128) % 192
            span = slice(row, row + 16)
            both = (own_ref[span] + got_ref[span].astype(F32)).astype(BF16)
            for j in range(8):
                piece_ref[8 * g + j, start - 48 * g : start - 48 * g + 16] = both[
                    :, 128 * j : 128 * j + 128
                ]


def mix_kernel(att_ref, weight_ref, out_ref):
    rows = [unfold_rows(att_ref[h].astype(F32)) for h in range(RANKS)]
    rows = jnp.concatenate(rows, axis=1).astype(BF16)
    out_ref[...] = dot_nn(rows, weight_ref[...]).astype(BF16)


def shift(value, axis, size, distance):
    return lax.ppermute(value, axis, [(i, (i + distance) % size) for i in range(size)])


def exchange(value, axis):
    return lax.all_to_all(value, axis, 0, 0, tiled=True)


def step(latents, out_grad, qkv_weight, out_weight):
    width = latents.shape[-1]
    z, yl, core = (lax.axis_index(a).astype(jnp.int32) for a in ("z", "yl", "core"))
    mine = latents.reshape(TOK, width)
    own = jnp.swapaxes(qkv_weight[0], 0, 1)
    other = shift(own, "yl", 2, 1)
    d7, d2, d1 = (shift(mine, "z", 8, d) for d in (7, 2, 1))
    pair0 = jnp.concatenate([mine, d7], axis=0)
    pair1 = jnp.concatenate([d1, d2], axis=0)
    pair2 = shift(pair0, "z", 8, -2)
    pair3 = shift(pair1, "z", 8, 2)
    tokens = (pair0, pair1, pair2, pair3)
    distance = jnp.array([0, 7, 1, 2, 6, 5, 3, 4], jnp.int32)
    rows = ((z - distance) % 8).astype(jnp.int32)
    place = jnp.stack([yl, core])

    (token_grad,) = call(
        token_grad_kernel, [((RANKS, 40, 128), BF16)], n_in=2, flops=2 * TOK * width * width
    )(out_grad.reshape(TOK, width), out_weight)
    band_grad = exchange(token_grad, HEAD)

    kv, query, swap, far, near, far2, near2 = call(
        project_kernel,
        [((8, TOK, 128), BF16), ((8, TOK, HD), BF16), ((8, TOK, 3 * HD), BF16)]
        + [((4, TOK, 128), BF16)] * 4,
        scratch=[pltpu.VMEM((8, TOK, 128), F32)] * 2,
        smem=(0,),
        n_in=7,
        flops=2 * 1152 * 192 * width,
    )(jnp.concatenate([rows, core.reshape(1)]), *tokens, own, other)
    far, near = send_far(far), shift(near, "core", 2, 1)
    far2, near2 = send_far(far2, 1), send_near(near2, 1)
    swapped = shift(swap, "yl", 2, 1)
    attended, dq, dkv, grad_far, grad_near = call(
        attend_kernel,
        [
            ((RANKS, 40, 128), BF16),
            ((RANKS, TOK, HD), F32),
            ((RANKS, TOK, 128), F32),
            ((8, TOK, 128), BF16),
            ((8, TOK, 128), BF16),
        ],
        scratch=[
            pltpu.VMEM((RANKS, TOK, 128), F32),
            pltpu.VMEM((RANKS, TOK, HD), F32),
            pltpu.VMEM((RANKS, TOK, 128), F32),
            pltpu.VMEM((RANKS, TOK, 128), F32),
        ],
        smem=(0,),
        n_in=9,
        flops=8 * 6 * 2 * 144 * 576 * 128,
    )(place, kv, query, swapped, band_grad, far, near, far2, near2)
    grad_far, grad_near = send_far(grad_far), shift(grad_near, "core", 2, 1)
    token_att = exchange(attended, HEAD)

    pg_mine, pg_swap = call(
        combine_kernel,
        [((8, TOK, 3 * HD), BF16), ((8, TOK, 3 * HD), BF16)],
        scratch=[pltpu.VMEM((RANKS, TOK, 3 * HD), F32)],
        smem=(0,),
        n_in=5,
        flops=1 << 20,
    )(place, dq, dkv, grad_far, grad_near)
    pg_got = shift(pg_swap, "yl", 2, 1)
    grads = []
    for pg, dtype in ((pg_mine, F32), (pg_got, BF16)):
        grads += call(
            weight_grad_kernel,
            [((3 * HD, width), dtype)],
            smem=(0,),
            n_in=6,
            flops=2 * 576 * 192 * width,
        )(rows, pg, *tokens)
    grad_got = shift(grads[1], "yl", 2, 1)
    (pieces,) = call(piece_kernel, [((32, 48, 128), BF16)], n_in=2, flops=1 << 20)(
        grads[0], grad_got
    )
    pieces = exchange(pieces, LON)
    reach = (5, 4, 3, 2, 6, 7, 1, 0)
    shares = call(
        share_kernel,
        [((2 * TOK, width), BF16)] * 2 + [((TOK, width), BF16)] * 4,
        smem=(0,),
        n_in=5,
        flops=2 * 576 * 384 * width,
    )(((z + jnp.array(reach, jnp.int32)) % 8).astype(jnp.int32), pg_mine, pg_got, own, other)
    down, up, s6, s7, s1, s0 = shares
    down, up = shift(down, "z", 8, -2), shift(up, "z", 8, 2)
    s7 = (s7.astype(F32) + down[:TOK].astype(F32)).astype(BF16)
    s6 = (s6.astype(F32) + down[TOK:].astype(F32)).astype(BF16)
    s1 = (s1.astype(F32) + up[:TOK].astype(F32)).astype(BF16)
    shares = [shift(s6, "z", 8, -2), shift(s7, "z", 8, -1)]
    shares = [s0, up[TOK:], shift(s1, "z", 8, 1)] + shares
    summed = jnp.sum(pieces.astype(F32), axis=0).astype(BF16)
    copies = exchange(jnp.broadcast_to(summed[None], (32, 48, 128)), LON)
    (mixed,) = call(mix_kernel, [((TOK, width), BF16)], n_in=2, flops=2 * TOK * width * width)(
        token_att, out_weight.reshape(width, width)
    )
    latent_grad = sum(s.astype(F32) for s in shares).astype(BF16)
    grad = copies.reshape(4, 8, 48, 128).transpose(0, 2, 1, 3).reshape(3 * HD, width)
    qkv_grad = jnp.swapaxes(grad, 0, 1).astype(F32)[None]
    return mixed.reshape(latents.shape), latent_grad.reshape(latents.shape), qkv_grad


def send_far(value, turn=0):
    routes = [
        (2 * i + j, 2 * ((i + (1 if i % 2 else -1)) % 32) + (j ^ turn))
        for i in range(32)
        for j in range(2)
    ]
    return lax.ppermute(value, LON + ("yl",), routes)


def send_near(value, turn=0):
    routes = [(2 * i + j, 2 * (i ^ 1) + (j ^ turn)) for i in range(32) for j in range(2)]
    return lax.ppermute(value, LON + ("yl",), routes)


def solution(mesh):
    split = Mesh(mesh.devices.reshape(4, 4, 2, 8, 2), LON + HEAD)
    rows = P(None, HEAD, LON, None)
    return jax.shard_map(
        step,
        mesh=split,
        in_specs=(rows, rows, P(HEAD, None, None), P()),
        out_specs=(rows, rows, P(HEAD, None, None)),
        check_vma=False,
    )
```

```python
import jax
import jax.numpy as jnp
from jax import lax
from jax.experimental import pallas as pl
from jax.experimental.pallas import tpu as pltpu
from jax.sharding import Mesh, PartitionSpec as P

HD = 64
RANKS = 16
TOK = 72
HEAD = ("z", "yl")
LON = ("x", "yh", "core")
F32 = jnp.float32
BF16 = jnp.bfloat16


def dot_nt(a, b):
    return lax.dot_general(a, b, (((1,), (1,)), ((), ())), preferred_element_type=F32)


def dot_nn(a, b):
    return lax.dot_general(a, b, (((1,), (0,)), ((), ())), preferred_element_type=F32)


def dot_tn(a, b):
    return lax.dot_general(a, b, (((0,), (0,)), ((), ())), preferred_element_type=F32)


def call(body, outs, scratch=(), smem=(), n_in=1, flops=0, moved=0):
    specs = [
        pl.BlockSpec(memory_space=pltpu.SMEM if i in smem else pltpu.VMEM) for i in range(n_in)
    ]
    return pl.pallas_call(
        body,
        out_shape=[jax.ShapeDtypeStruct(s, d) for s, d in outs],
        in_specs=specs,
        out_specs=[pl.BlockSpec(memory_space=pltpu.VMEM) for _ in outs],
        scratch_shapes=list(scratch),
        cost_estimate=pl.CostEstimate(flops=flops, bytes_accessed=moved, transcendentals=0),
        compiler_params=pltpu.CompilerParams(vmem_limit_bytes=56 << 20),
    )


def low_half(shape):
    return lax.broadcasted_iota(jnp.int32, shape, len(shape) - 2) % 8 < 4


def pack_pair(value):
    half = value.shape[0] // 2
    groups = value.reshape(2, half * TOK // 8, 8, 128)
    first, second = groups[0], groups[1]
    low = low_half(first.shape)
    west = jnp.where(low, first, pltpu.roll(second, 4, 1))
    east = jnp.where(low, pltpu.roll(first, 4, 1), second)
    return west.reshape(half, TOK, 128), east.reshape(half, TOK, 128)


def unpack_pair(west, east):
    half = west.shape[0]
    west = west.reshape(half * TOK // 8, 8, 128)
    east = east.reshape(half * TOK // 8, 8, 128)
    low = low_half(west.shape)
    first = jnp.where(low, west, pltpu.roll(east, 4, 1))
    second = jnp.where(low, pltpu.roll(west, 4, 1), east)
    return first.reshape(half, TOK, 128), second.reshape(half, TOK, 128)


def fold_rows(value):
    rest = jnp.concatenate([value[40:], jnp.zeros((8, HD), F32)], axis=0)
    return jnp.concatenate([value[:40], rest], axis=1)


def unfold_rows(value):
    return jnp.concatenate([value[:, :HD], value[:32, HD:]], axis=0)


def turned(ref):
    return jnp.concatenate([ref[HD : 3 * HD], ref[0:HD]], axis=0)


def token_grad_kernel(grad_ref, weight_ref, out_ref):
    for pair in range(RANKS // 2):
        rows = weight_ref[2 * pair : 2 * pair + 2].reshape(2 * HD, -1)
        both = dot_nt(grad_ref[...], rows)
        out_ref[2 * pair] = fold_rows(both[:, :HD]).astype(BF16)
        out_ref[2 * pair + 1] = fold_rows(both[:, HD:]).astype(BF16)


def project_kernel(
    table_ref, t0_ref, t1_ref, t2_ref, t3_ref, own_ref, other_ref,
    kv_ref, q_ref, swap_ref, far_ref, near_ref, far2_ref, near2_ref,
    kv32, kv32b,
):
    first_core = table_ref[8] == 0
    own, other = turned(own_ref), turned(other_ref)
    for chunk, (a_ref, b_ref) in enumerate(((t0_ref, t1_ref), (t2_ref, t3_ref))):
        rows = jnp.concatenate([a_ref[...], b_ref[...]], axis=0)
        proj = dot_nt(rows, own).astype(BF16).astype(F32)
        proj2 = dot_nt(rows, other).astype(BF16).astype(F32)
        for part in range(4):
            row = table_ref[chunk * 4 + part]
            piece = proj[part * TOK : (part + 1) * TOK]
            kv32[row] = piece[:, :128]
            kv_ref[row] = piece[:, :128].astype(BF16)
            q_ref[row] = piece[:, 128:].astype(BF16)
            piece = proj2[part * TOK : (part + 1) * TOK]
            kv32b[row] = piece[:, :128]
            swap_ref[row] = piece.astype(BF16)
    west, east = pack_pair(kv32[...])
    far_ref[...] = jnp.where(first_core, west, east).astype(BF16)
    near_ref[...] = jnp.where(first_core, east, west).astype(BF16)
    west, east = pack_pair(kv32b[...])
    far2_ref[...] = jnp.where(first_core, west, east).astype(BF16)
    near2_ref[...] = jnp.where(first_core, east, west).astype(BF16)


def attend_kernel(
    place_ref, kv_ref, q_ref, swapped_ref, grad_ref, far_ref, near_ref, far2_ref, near2_ref,
    out_ref, dq_ref, dkv_ref, to_far_ref, to_near_ref,
    keys, queries, halo, dhalo,
):
    scale = HD ** (-0.5)
    yl = place_ref[0]
    first_core = place_ref[1] == 0
    far, near = far_ref[...].astype(F32), near_ref[...].astype(F32)
    side = unpack_pair(jnp.where(first_core, near, far), jnp.where(first_core, far, near))
    far, near = far2_ref[...].astype(F32), near2_ref[...].astype(F32)
    side2 = unpack_pair(jnp.where(first_core, near, far), jnp.where(first_core, far, near))
    for row in range(8):
        mine, theirs = 2 * row + yl, 2 * row + 1 - yl
        keys[mine] = kv_ref[row].astype(F32)
        queries[mine] = q_ref[row].astype(F32)
        both = swapped_ref[row].astype(F32)
        keys[theirs] = both[:, :128]
        queries[theirs] = both[:, 128:]
        halo[mine] = side[row // 4][row % 4]
        halo[theirs] = side2[row // 4][row % 4]
    zeros = jnp.zeros((2 * TOK, HD), F32)
    windows = RANKS // 2
    for w in range(windows):
        lo, hi = max(2 * w - 1, 0), min(2 * w + 3, RANKS)
        count = (hi - lo) * TOK
        query = queries[2 * w : 2 * w + 2].reshape(2 * TOK, HD) * scale
        outer = jnp.concatenate(
            [unfold_rows(grad_ref[2 * w + i].astype(F32)) for i in range(2)], axis=0
        )
        lhs = jnp.concatenate(
            [
                jnp.concatenate([query, zeros], axis=1),
                jnp.concatenate([zeros, outer], axis=1),
            ],
            axis=0,
        ).astype(BF16)
        pairs = jnp.concatenate(
            [keys[lo:hi].reshape(count, 128), halo[lo:hi].reshape(count, 128)], axis=0
        ).astype(BF16)
        both = dot_nt(lhs, pairs)
        score, prob_grad = both[: 2 * TOK], both[2 * TOK :]
        powers = jnp.exp(score - jnp.max(score, axis=-1, keepdims=True))
        probs = powers * (1.0 / jnp.sum(powers, axis=-1, keepdims=True))
        centre = jnp.sum(probs * prob_grad, axis=-1, keepdims=True)
        score_grad = (probs * (prob_grad - centre)).astype(BF16)
        stack = jnp.concatenate([score_grad, probs.astype(BF16)], axis=0)
        mixed = dot_nn(stack, pairs)
        dq_ref[2 * w : 2 * w + 2] = (mixed[: 2 * TOK, :HD] * scale).reshape(2, TOK, HD)
        for i in range(2):
            rows = mixed[(2 + i) * TOK : (3 + i) * TOK, HD:]
            out_ref[2 * w + i] = fold_rows(rows).astype(BF16)
        grads = dot_tn(stack, lhs)
        own = grads[:count].reshape(hi - lo, TOK, 128)
        side = grads[count:].reshape(hi - lo, TOK, 128)
        for i, rank in enumerate(range(lo, hi)):
            seen = w > 0 and rank <= 2 * w
            if seen:
                dkv_ref[rank] += own[i]
                dhalo[rank] += side[i]
            else:
                dkv_ref[rank] = own[i]
                dhalo[rank] = side[i]
    to_e, to_w = pack_pair(dhalo[...])
    to_far_ref[...] = jnp.where(first_core, to_w, to_e).astype(BF16)
    to_near_ref[...] = jnp.where(first_core, to_e, to_w).astype(BF16)


def combine_kernel(
    place_ref, dq_ref, dkv_ref, far_ref, near_ref, pg_ref, mine_ref, swap_ref, pg32
):
    yl = place_ref[0]
    first_core = place_ref[1] == 0
    far, near = far_ref[...].astype(F32), near_ref[...].astype(F32)
    first, second = unpack_pair(jnp.where(first_core, far, near), jnp.where(first_core, near, far))
    for half, add in ((0, first), (1, second)):
        span = slice(8 * half, 8 * half + 8)
        pg32[span, :, 0:128] = dkv_ref[span] + add
        pg32[span, :, 128:192] = dq_ref[span]
    pg_ref[...] = pg32[...].astype(BF16)
    for row in range(8):
        mine_ref[row] = pg32[2 * row + yl].astype(BF16)
        swap_ref[row] = pg32[2 * row + 1 - yl].astype(BF16)


def share_kernel(table_ref, mine_ref, got_ref, own_ref, other_ref, *out_refs):
    own, other = turned(own_ref), turned(other_ref)
    for chunk in range(2):
        picks = [table_ref[4 * chunk + i] for i in range(4)]
        rows = jnp.concatenate([mine_ref[p].astype(F32) for p in picks], axis=0).astype(BF16)
        rows2 = jnp.concatenate([got_ref[p].astype(F32) for p in picks], axis=0).astype(BF16)
        part = (dot_nn(rows, own) + dot_nn(rows2, other)).astype(BF16)
        if chunk == 0:
            out_refs[0][...] = part[: 2 * TOK]
            out_refs[1][...] = part[2 * TOK :]
        else:
            for i in range(4):
                out_refs[2 + i][...] = part[i * TOK : (i + 1) * TOK]


def weight_grad_kernel(table_ref, pg_ref, *refs):
    total, piece_ref = None, refs[8]
    for chunk in range(4):
        rows = jnp.concatenate(
            [pg_ref[table_ref[4 * chunk + i]].astype(F32) for i in range(4)], axis=0
        ).astype(BF16)
        source = jnp.concatenate([refs[2 * chunk][...], refs[2 * chunk + 1][...]], axis=0)
        part = dot_tn(rows, source)
        total = part if total is None else total + part
    total = jnp.concatenate([total[128:192], total[0:128]], axis=0).astype(BF16)
    for g in range(4):
        for j in range(8):
            piece_ref[8 * g + j] = total[48 * g : 48 * g + 48, 128 * j : 128 * j + 128]


def mix_kernel(att_ref, weight_ref, out_ref):
    rows = [unfold_rows(att_ref[h].astype(F32)) for h in range(RANKS)]
    rows = jnp.concatenate(rows, axis=1).astype(BF16)
    out_ref[...] = dot_nn(rows, weight_ref[...]).astype(BF16)


def shift(value, axis, size, distance):
    return lax.ppermute(value, axis, [(i, (i + distance) % size) for i in range(size)])


def exchange(value, axis):
    return lax.all_to_all(value, axis, 0, 0, tiled=True)


def step(latents, out_grad, qkv_weight, out_weight):
    width = latents.shape[-1]
    z, yl, core = (lax.axis_index(a).astype(jnp.int32) for a in ("z", "yl", "core"))
    mine = latents.reshape(TOK, width)
    own = jnp.swapaxes(qkv_weight[0], 0, 1)
    other = shift(own, "yl", 2, 1)
    d7, d2, d1 = (shift(mine, "z", 8, d) for d in (7, 2, 1))
    pair0 = jnp.concatenate([mine, d7], axis=0)
    pair1 = jnp.concatenate([d1, d2], axis=0)
    pair2 = shift(pair0, "z", 8, -2)
    pair3 = shift(pair1, "z", 8, 2)
    tokens = (pair0, pair1, pair2, pair3)
    distance = jnp.array([0, 7, 1, 2, 6, 5, 3, 4], jnp.int32)
    late0, late1 = shift(pair0, "yl", 2, 1), shift(pair1, "yl", 2, 1)
    late2, late3 = shift(pair2, "yl", 2, 1), shift(late1, "z", 8, 2)
    rows = ((z - distance) % 8).astype(jnp.int32)
    place = jnp.stack([yl, core])

    (token_grad,) = call(
        token_grad_kernel, [((RANKS, 40, 128), BF16)], n_in=2, flops=2 * TOK * width * width
    )(out_grad.reshape(TOK, width), out_weight)
    band_grad = exchange(token_grad, HEAD)

    kv, query, swap, far, near, far2, near2 = call(
        project_kernel,
        [((8, TOK, 128), BF16), ((8, TOK, HD), BF16), ((8, TOK, 3 * HD), BF16)]
        + [((4, TOK, 128), BF16)] * 4,
        scratch=[pltpu.VMEM((8, TOK, 128), F32)] * 2,
        smem=(0,),
        n_in=7,
        flops=2 * 1152 * 192 * width,
    )(jnp.concatenate([rows, core.reshape(1)]), *tokens, own, other)
    far, near = send_far(far), shift(near, "core", 2, 1)
    far2, near2 = send_far(far2, 1), send_near(near2, 1)
    swapped = shift(swap, "yl", 2, 1)
    attended, dq, dkv, grad_far, grad_near = call(
        attend_kernel,
        [
            ((RANKS, 40, 128), BF16),
            ((RANKS, TOK, HD), F32),
            ((RANKS, TOK, 128), F32),
            ((8, TOK, 128), BF16),
            ((8, TOK, 128), BF16),
        ],
        scratch=[
            pltpu.VMEM((RANKS, TOK, 128), F32),
            pltpu.VMEM((RANKS, TOK, HD), F32),
            pltpu.VMEM((RANKS, TOK, 128), F32),
            pltpu.VMEM((RANKS, TOK, 128), F32),
        ],
        smem=(0,),
        n_in=9,
        flops=8 * 6 * 2 * 144 * 576 * 128,
    )(place, kv, query, swapped, band_grad, far, near, far2, near2)
    grad_far, grad_near = send_far(grad_far), shift(grad_near, "core", 2, 1)
    token_att = exchange(attended, HEAD)

    pg, pg_mine, pg_swap = call(
        combine_kernel,
        [((RANKS, TOK, 3 * HD), BF16), ((8, TOK, 3 * HD), BF16), ((8, TOK, 3 * HD), BF16)],
        scratch=[pltpu.VMEM((RANKS, TOK, 3 * HD), F32)],
        smem=(0,),
        n_in=5,
        flops=1 << 20,
    )(place, dq, dkv, grad_far, grad_near)
    pg_got = shift(pg_swap, "yl", 2, 1)
    (pieces,) = call(
        weight_grad_kernel,
        [((32, 48, 128), BF16)],
        smem=(0,),
        n_in=10,
        flops=2 * 1152 * 192 * width,
    )(
        jnp.concatenate([2 * rows + yl, 2 * rows + 1 - yl]).astype(jnp.int32),
        pg, *tokens, late0, late1, late2, late3,
    )
    pieces = exchange(pieces, LON)
    reach = (5, 4, 3, 2, 6, 7, 1, 0)
    shares = call(
        share_kernel,
        [((2 * TOK, width), BF16)] * 2 + [((TOK, width), BF16)] * 4,
        smem=(0,),
        n_in=5,
        flops=2 * 576 * 384 * width,
    )(((z + jnp.array(reach, jnp.int32)) % 8).astype(jnp.int32), pg_mine, pg_got, own, other)
    down, up, s6, s7, s1, s0 = shares
    down, up = shift(down, "z", 8, -2), shift(up, "z", 8, 2)
    s7 = (s7.astype(F32) + down[:TOK].astype(F32)).astype(BF16)
    s6 = (s6.astype(F32) + down[TOK:].astype(F32)).astype(BF16)
    s1 = (s1.astype(F32) + up[:TOK].astype(F32)).astype(BF16)
    shares = [shift(s6, "z", 8, -2), shift(s7, "z", 8, -1)]
    shares = [s0, up[TOK:], shift(s1, "z", 8, 1)] + shares
    summed = jnp.sum(pieces.astype(F32), axis=0).astype(BF16)
    copies = exchange(jnp.broadcast_to(summed[None], (32, 48, 128)), LON)
    (mixed,) = call(mix_kernel, [((TOK, width), BF16)], n_in=2, flops=2 * TOK * width * width)(
        token_att, out_weight.reshape(width, width)
    )
    latent_grad = sum(s.astype(F32) for s in shares).astype(BF16)
    grad = copies.reshape(4, 8, 48, 128).transpose(0, 2, 1, 3).reshape(3 * HD, width)
    qkv_grad = jnp.swapaxes(grad, 0, 1).astype(F32)[None]
    return mixed.reshape(latents.shape), latent_grad.reshape(latents.shape), qkv_grad


def send_far(value, turn=0):
    routes = [
        (2 * i + j, 2 * ((i + (1 if i % 2 else -1)) % 32) + (j ^ turn))
        for i in range(32)
        for j in range(2)
    ]
    return lax.ppermute(value, LON + ("yl",), routes)


def send_near(value, turn=0):
    routes = [(2 * i + j, 2 * (i ^ 1) + (j ^ turn)) for i in range(32) for j in range(2)]
    return lax.ppermute(value, LON + ("yl",), routes)


def solution(mesh):
    split = Mesh(mesh.devices.reshape(4, 4, 2, 8, 2), LON + HEAD)
    rows = P(None, HEAD, LON, None)
    return jax.shard_map(
        step,
        mesh=split,
        in_specs=(rows, rows, P(HEAD, None, None), P()),
        out_specs=(rows, rows, P(HEAD, None, None)),
        check_vma=False,
    )
```

```python
import jax
import jax.numpy as jnp
from jax import lax
from jax.experimental import pallas as pl
from jax.experimental.pallas import tpu as pltpu
from jax.sharding import Mesh, PartitionSpec as P

HD = 64
RANKS = 16
TOK = 72
HEAD = ("z", "yl")
LON = ("x", "yh", "core")
F32 = jnp.float32
BF16 = jnp.bfloat16


DISTANCE = (0, 7, 1, 2, 6, 5, 3, 4)


def dot_nt(a, b):
    return lax.dot_general(a, b, (((1,), (1,)), ((), ())), preferred_element_type=F32)


def dot_nn(a, b):
    return lax.dot_general(a, b, (((1,), (0,)), ((), ())), preferred_element_type=F32)


def dot_tn(a, b):
    return lax.dot_general(a, b, (((0,), (0,)), ((), ())), preferred_element_type=F32)


def call(body, outs, scratch=(), smem=(), n_in=1, flops=0, moved=0):
    specs = [
        pl.BlockSpec(memory_space=pltpu.SMEM if i in smem else pltpu.VMEM) for i in range(n_in)
    ]
    return pl.pallas_call(
        body,
        out_shape=[jax.ShapeDtypeStruct(s, d) for s, d in outs],
        in_specs=specs,
        out_specs=[pl.BlockSpec(memory_space=pltpu.VMEM) for _ in outs],
        scratch_shapes=list(scratch),
        cost_estimate=pl.CostEstimate(flops=flops, bytes_accessed=moved, transcendentals=0),
        compiler_params=pltpu.CompilerParams(vmem_limit_bytes=12 << 20),
    )


def low_half(shape):
    return lax.broadcasted_iota(jnp.int32, shape, len(shape) - 2) % 8 < 4


def pack_pair(value):
    half = value.shape[0] // 2
    groups = value.reshape(2, half * TOK // 8, 8, 128)
    first, second = groups[0], groups[1]
    low = low_half(first.shape)
    west = jnp.where(low, first, pltpu.roll(second, 4, 1))
    east = jnp.where(low, pltpu.roll(first, 4, 1), second)
    return west.reshape(half, TOK, 128), east.reshape(half, TOK, 128)


def unpack_pair(west, east):
    half = west.shape[0]
    west = west.reshape(half * TOK // 8, 8, 128)
    east = east.reshape(half * TOK // 8, 8, 128)
    low = low_half(west.shape)
    first = jnp.where(low, west, pltpu.roll(east, 4, 1))
    second = jnp.where(low, pltpu.roll(west, 4, 1), east)
    return first.reshape(half, TOK, 128), second.reshape(half, TOK, 128)


def fold_rows(value):
    rest = jnp.concatenate([value[40:], jnp.zeros((8, HD), F32)], axis=0)
    return jnp.concatenate([value[:40], rest], axis=1)


def unfold_rows(value):
    return jnp.concatenate([value[:, :HD], value[:32, HD:]], axis=0)


def turned(ref):
    return jnp.concatenate([ref[HD : 3 * HD], ref[0:HD]], axis=0)


def token_grad_kernel(grad_ref, weight_ref, out_ref):
    for pair in range(RANKS // 2):
        rows = weight_ref[2 * pair : 2 * pair + 2].reshape(2 * HD, -1)
        both = dot_nt(grad_ref[...], rows)
        out_ref[2 * pair] = fold_rows(both[:, :HD]).astype(BF16)
        out_ref[2 * pair + 1] = fold_rows(both[:, HD:]).astype(BF16)


def project_kernel(
    place_ref, t0_ref, t1_ref, t2_ref, t3_ref, own_ref, other_ref,
    kv_ref, q_ref, swap_ref, far_ref, near_ref, far2_ref, near2_ref,
    kv32, kv32b,
):
    first_core = place_ref[2] == 0
    own, other = turned(own_ref), turned(other_ref)
    for chunk, (a_ref, b_ref) in enumerate(((t0_ref, t1_ref), (t2_ref, t3_ref))):
        rows = jnp.concatenate([a_ref[...], b_ref[...]], axis=0)
        proj = dot_nt(rows, own).astype(BF16).astype(F32)
        proj2 = dot_nt(rows, other).astype(BF16).astype(F32)
        for part in range(4):
            row = lax.rem(place_ref[0] + 8 - DISTANCE[chunk * 4 + part], 8)
            piece = proj[part * TOK : (part + 1) * TOK]
            kv32[row] = piece[:, :128]
            kv_ref[row] = piece[:, :128].astype(BF16)
            q_ref[row] = piece[:, 128:].astype(BF16)
            piece = proj2[part * TOK : (part + 1) * TOK]
            kv32b[row] = piece[:, :128]
            swap_ref[row] = piece.astype(BF16)
    west, east = pack_pair(kv32[...])
    far_ref[...] = jnp.where(first_core, west, east).astype(BF16)
    near_ref[...] = jnp.where(first_core, east, west).astype(BF16)
    west, east = pack_pair(kv32b[...])
    far2_ref[...] = jnp.where(first_core, west, east).astype(BF16)
    near2_ref[...] = jnp.where(first_core, east, west).astype(BF16)


def attend_kernel(
    place_ref, kv_ref, q_ref, swapped_ref, grad_ref, far_ref, near_ref, far2_ref, near2_ref,
    out_ref, dq_ref, dkv_ref, to_far_ref, to_near_ref,
    keys, queries, halo, dhalo,
):
    scale = HD ** (-0.5)
    yl = place_ref[1]
    first_core = place_ref[2] == 0
    far, near = far_ref[...].astype(F32), near_ref[...].astype(F32)
    side = unpack_pair(jnp.where(first_core, near, far), jnp.where(first_core, far, near))
    far, near = far2_ref[...].astype(F32), near2_ref[...].astype(F32)
    side2 = unpack_pair(jnp.where(first_core, near, far), jnp.where(first_core, far, near))
    for row in range(8):
        mine, theirs = 2 * row + yl, 2 * row + 1 - yl
        keys[mine] = kv_ref[row].astype(F32)
        queries[mine] = q_ref[row].astype(F32)
        both = swapped_ref[row].astype(F32)
        keys[theirs] = both[:, :128]
        queries[theirs] = both[:, 128:]
        halo[mine] = side[row // 4][row % 4]
        halo[theirs] = side2[row // 4][row % 4]
    zeros = jnp.zeros((2 * TOK, HD), F32)
    windows = RANKS // 2
    for w in range(windows):
        lo, hi = max(2 * w - 1, 0), min(2 * w + 3, RANKS)
        count = (hi - lo) * TOK
        query = queries[2 * w : 2 * w + 2].reshape(2 * TOK, HD) * scale
        outer = jnp.concatenate(
            [unfold_rows(grad_ref[2 * w + i].astype(F32)) for i in range(2)], axis=0
        )
        lhs = jnp.concatenate(
            [
                jnp.concatenate([query, zeros], axis=1),
                jnp.concatenate([zeros, outer], axis=1),
            ],
            axis=0,
        ).astype(BF16)
        pairs = jnp.concatenate(
            [keys[lo:hi].reshape(count, 128), halo[lo:hi].reshape(count, 128)], axis=0
        ).astype(BF16)
        both = dot_nt(lhs, pairs)
        score, prob_grad = both[: 2 * TOK], both[2 * TOK :]
        powers = jnp.exp(score - jnp.max(score, axis=-1, keepdims=True))
        probs = powers * (1.0 / jnp.sum(powers, axis=-1, keepdims=True))
        centre = jnp.sum(probs * prob_grad, axis=-1, keepdims=True)
        score_grad = (probs * (prob_grad - centre)).astype(BF16)
        stack = jnp.concatenate([score_grad, probs.astype(BF16)], axis=0)
        mixed = dot_nn(stack, pairs)
        dq_ref[2 * w : 2 * w + 2] = (mixed[: 2 * TOK, :HD] * scale).reshape(2, TOK, HD)
        for i in range(2):
            rows = mixed[(2 + i) * TOK : (3 + i) * TOK, HD:]
            out_ref[2 * w + i] = fold_rows(rows).astype(BF16)
        grads = dot_tn(stack, lhs)
        own = grads[:count].reshape(hi - lo, TOK, 128)
        side = grads[count:].reshape(hi - lo, TOK, 128)
        for i, rank in enumerate(range(lo, hi)):
            seen = w > 0 and rank <= 2 * w
            if seen:
                dkv_ref[rank] += own[i]
                dhalo[rank] += side[i]
            else:
                dkv_ref[rank] = own[i]
                dhalo[rank] = side[i]
    to_e, to_w = pack_pair(dhalo[...])
    to_far_ref[...] = jnp.where(first_core, to_w, to_e).astype(BF16)
    to_near_ref[...] = jnp.where(first_core, to_e, to_w).astype(BF16)


def combine_kernel(
    place_ref, dq_ref, dkv_ref, far_ref, near_ref, pg_ref, mine_ref, swap_ref, pg32
):
    yl = place_ref[1]
    first_core = place_ref[2] == 0
    far, near = far_ref[...].astype(F32), near_ref[...].astype(F32)
    first, second = unpack_pair(jnp.where(first_core, far, near), jnp.where(first_core, near, far))
    for half, add in ((0, first), (1, second)):
        span = slice(8 * half, 8 * half + 8)
        pg32[span, :, 0:128] = dkv_ref[span] + add
        pg32[span, :, 128:192] = dq_ref[span]
    pg_ref[...] = pg32[...].astype(BF16)
    for row in range(8):
        mine_ref[row] = pg32[2 * row + yl].astype(BF16)
        swap_ref[row] = pg32[2 * row + 1 - yl].astype(BF16)


def share_kernel(place_ref, mine_ref, got_ref, own_ref, other_ref, *out_refs):
    own, other = turned(own_ref), turned(other_ref)
    for chunk in range(2):
        reach = (6, 7, 1, 0) if chunk else (5, 4, 3, 2)
        picks = [lax.rem(place_ref[0] + r, 8) for r in reach]
        rows = jnp.concatenate([mine_ref[p].astype(F32) for p in picks], axis=0).astype(BF16)
        rows2 = jnp.concatenate([got_ref[p].astype(F32) for p in picks], axis=0).astype(BF16)
        part = (dot_nn(rows, own) + dot_nn(rows2, other)).astype(BF16)
        if chunk == 0:
            out_refs[0][...] = part[: 2 * TOK]
            out_refs[1][...] = part[2 * TOK :]
        else:
            for i in range(4):
                out_refs[2 + i][...] = part[i * TOK : (i + 1) * TOK]


def weight_grad_kernel(place_ref, pg_ref, *refs):
    total, piece_ref = None, refs[8]
    yl = place_ref[1]
    for chunk in range(4):
        parity = yl if chunk < 2 else 1 - yl
        near = DISTANCE[4 * (chunk % 2) : 4 * (chunk % 2) + 4]
        ranks = [2 * lax.rem(place_ref[0] + 8 - d, 8) + parity for d in near]
        rows = jnp.concatenate([pg_ref[r].astype(F32) for r in ranks], axis=0).astype(BF16)
        source = jnp.concatenate([refs[2 * chunk][...], refs[2 * chunk + 1][...]], axis=0)
        part = dot_tn(rows, source)
        total = part if total is None else total + part
    total = jnp.concatenate([total[128:192], total[0:128]], axis=0).astype(BF16)
    for g in range(4):
        for j in range(8):
            piece_ref[8 * g + j] = total[48 * g : 48 * g + 48, 128 * j : 128 * j + 128]


def mix_kernel(att_ref, weight_ref, out_ref):
    rows = [unfold_rows(att_ref[h].astype(F32)) for h in range(RANKS)]
    rows = jnp.concatenate(rows, axis=1).astype(BF16)
    out_ref[...] = dot_nn(rows, weight_ref[...]).astype(BF16)


def shift(value, axis, size, distance):
    return lax.ppermute(value, axis, [(i, (i + distance) % size) for i in range(size)])


def exchange(value, axis):
    return lax.all_to_all(value, axis, 0, 0, tiled=True)


def step(latents, out_grad, qkv_weight, out_weight):
    width = latents.shape[-1]
    z, yl, core = (lax.axis_index(a).astype(jnp.int32) for a in ("z", "yl", "core"))
    mine = latents.reshape(TOK, width)
    own = jnp.swapaxes(qkv_weight[0], 0, 1)
    other = shift(own, "yl", 2, 1)
    d7, d2, d1 = (shift(mine, "z", 8, d) for d in (7, 2, 1))
    pair0 = jnp.concatenate([mine, d7], axis=0)
    pair1 = jnp.concatenate([d1, d2], axis=0)
    pair2 = shift(pair0, "z", 8, -2)
    pair3 = shift(pair1, "z", 8, 2)
    tokens = (pair0, pair1, pair2, pair3)
    late0, late1 = shift(pair0, "yl", 2, 1), shift(pair1, "yl", 2, 1)
    late2, late3 = shift(pair2, "yl", 2, 1), shift(late1, "z", 8, 2)
    place = jnp.stack([z, yl, core])

    (token_grad,) = call(
        token_grad_kernel, [((RANKS, 40, 128), BF16)], n_in=2, flops=2 * TOK * width * width
    )(out_grad.reshape(TOK, width), out_weight)
    band_grad = exchange(token_grad, HEAD)

    kv, query, swap, far, near, far2, near2 = call(
        project_kernel,
        [((8, TOK, 128), BF16), ((8, TOK, HD), BF16), ((8, TOK, 3 * HD), BF16)]
        + [((4, TOK, 128), BF16)] * 4,
        scratch=[pltpu.VMEM((8, TOK, 128), F32)] * 2,
        smem=(0,),
        n_in=7,
        flops=2 * 1152 * 192 * width,
    )(place, *tokens, own, other)
    far, near = send_far(far), shift(near, "core", 2, 1)
    far2, near2 = send_far(far2, 1), send_near(near2, 1)
    swapped = shift(swap, "yl", 2, 1)
    attended, dq, dkv, grad_far, grad_near = call(
        attend_kernel,
        [
            ((RANKS, 40, 128), BF16),
            ((RANKS, TOK, HD), F32),
            ((RANKS, TOK, 128), F32),
            ((8, TOK, 128), BF16),
            ((8, TOK, 128), BF16),
        ],
        scratch=[
            pltpu.VMEM((RANKS, TOK, 128), F32),
            pltpu.VMEM((RANKS, TOK, HD), F32),
            pltpu.VMEM((RANKS, TOK, 128), F32),
            pltpu.VMEM((RANKS, TOK, 128), F32),
        ],
        smem=(0,),
        n_in=9,
        flops=8 * 6 * 2 * 144 * 576 * 128,
    )(place, kv, query, swapped, band_grad, far, near, far2, near2)
    grad_far, grad_near = send_far(grad_far), shift(grad_near, "core", 2, 1)
    token_att = exchange(attended, HEAD)

    pg, pg_mine, pg_swap = call(
        combine_kernel,
        [((RANKS, TOK, 3 * HD), BF16), ((8, TOK, 3 * HD), BF16), ((8, TOK, 3 * HD), BF16)],
        scratch=[pltpu.VMEM((RANKS, TOK, 3 * HD), F32)],
        smem=(0,),
        n_in=5,
        flops=1 << 20,
    )(place, dq, dkv, grad_far, grad_near)
    pg_got = shift(pg_swap, "yl", 2, 1)
    (pieces,) = call(
        weight_grad_kernel,
        [((32, 48, 128), BF16)],
        smem=(0,),
        n_in=10,
        flops=2 * 1152 * 192 * width,
    )(place, pg, *tokens, late0, late1, late2, late3)
    pieces = exchange(pieces, LON)
    shares = call(
        share_kernel,
        [((2 * TOK, width), BF16)] * 2 + [((TOK, width), BF16)] * 4,
        smem=(0,),
        n_in=5,
        flops=2 * 576 * 384 * width,
    )(place, pg_mine, pg_got, own, other)
    down, up, s6, s7, s1, s0 = shares
    down, up = shift(down, "z", 8, -2), shift(up, "z", 8, 2)
    s7 = (s7.astype(F32) + down[:TOK].astype(F32)).astype(BF16)
    s6 = (s6.astype(F32) + down[TOK:].astype(F32)).astype(BF16)
    s1 = (s1.astype(F32) + up[:TOK].astype(F32)).astype(BF16)
    shares = [shift(s6, "z", 8, -2), shift(s7, "z", 8, -1)]
    shares = [s0, up[TOK:], shift(s1, "z", 8, 1)] + shares
    summed = jnp.sum(pieces.astype(F32), axis=0).astype(BF16)
    copies = exchange(jnp.broadcast_to(summed[None], (32, 48, 128)), LON)
    (mixed,) = call(mix_kernel, [((TOK, width), BF16)], n_in=2, flops=2 * TOK * width * width)(
        token_att, out_weight.reshape(width, width)
    )
    latent_grad = sum(s.astype(F32) for s in shares).astype(BF16)
    grad = copies.reshape(4, 8, 48, 128).transpose(0, 2, 1, 3).reshape(3 * HD, width)
    qkv_grad = jnp.swapaxes(grad, 0, 1).astype(F32)[None]
    return mixed.reshape(latents.shape), latent_grad.reshape(latents.shape), qkv_grad


def send_far(value, turn=0):
    routes = [
        (2 * i + j, 2 * ((i + (1 if i % 2 else -1)) % 32) + (j ^ turn))
        for i in range(32)
        for j in range(2)
    ]
    return lax.ppermute(value, LON + ("yl",), routes)


def send_near(value, turn=0):
    routes = [(2 * i + j, 2 * (i ^ 1) + (j ^ turn)) for i in range(32) for j in range(2)]
    return lax.ppermute(value, LON + ("yl",), routes)


def solution(mesh):
    split = Mesh(mesh.devices.reshape(4, 4, 2, 8, 2), LON + HEAD)
    rows = P(None, HEAD, LON, None)
    return jax.shard_map(
        step,
        mesh=split,
        in_specs=(rows, rows, P(HEAD, None, None), P()),
        out_specs=(rows, rows, P(HEAD, None, None)),
        check_vma=False,
    )
```

```python
import jax
import jax.numpy as jnp
from jax import lax
from jax.experimental import pallas as pl
from jax.experimental.pallas import tpu as pltpu
from jax.sharding import Mesh, PartitionSpec as P

HD = 64
RANKS = 16
TOK = 72
HEAD = ("z", "yl")
LON = ("x", "yh", "core")
F32 = jnp.float32
BF16 = jnp.bfloat16


DISTANCE = (0, 7, 1, 2, 6, 5, 3, 4)


def dot_nt(a, b):
    return lax.dot_general(a, b, (((1,), (1,)), ((), ())), preferred_element_type=F32)


def dot_nn(a, b):
    return lax.dot_general(a, b, (((1,), (0,)), ((), ())), preferred_element_type=F32)


def dot_tn(a, b):
    return lax.dot_general(a, b, (((0,), (0,)), ((), ())), preferred_element_type=F32)


def call(body, outs, scratch=(), smem=(), n_in=1, flops=0, moved=0, grant=56):
    specs = [
        pl.BlockSpec(memory_space=pltpu.SMEM if i in smem else pltpu.VMEM) for i in range(n_in)
    ]
    return pl.pallas_call(
        body,
        out_shape=[jax.ShapeDtypeStruct(s, d) for s, d in outs],
        in_specs=specs,
        out_specs=[pl.BlockSpec(memory_space=pltpu.VMEM) for _ in outs],
        scratch_shapes=list(scratch),
        cost_estimate=pl.CostEstimate(flops=flops, bytes_accessed=moved, transcendentals=0),
        compiler_params=pltpu.CompilerParams(vmem_limit_bytes=grant << 20),
    )


def low_half(shape):
    return lax.broadcasted_iota(jnp.int32, shape, len(shape) - 2) % 8 < 4


def pack_pair(value):
    half = value.shape[0] // 2
    groups = value.reshape(2, half * TOK // 8, 8, 128)
    first, second = groups[0], groups[1]
    low = low_half(first.shape)
    west = jnp.where(low, first, pltpu.roll(second, 4, 1))
    east = jnp.where(low, pltpu.roll(first, 4, 1), second)
    return west.reshape(half, TOK, 128), east.reshape(half, TOK, 128)


def unpack_pair(west, east):
    half = west.shape[0]
    west = west.reshape(half * TOK // 8, 8, 128)
    east = east.reshape(half * TOK // 8, 8, 128)
    low = low_half(west.shape)
    first = jnp.where(low, west, pltpu.roll(east, 4, 1))
    second = jnp.where(low, pltpu.roll(west, 4, 1), east)
    return first.reshape(half, TOK, 128), second.reshape(half, TOK, 128)


def fold_rows(value):
    rest = jnp.concatenate([value[40:], jnp.zeros((8, HD), F32)], axis=0)
    return jnp.concatenate([value[:40], rest], axis=1)


def unfold_rows(value):
    return jnp.concatenate([value[:, :HD], value[:32, HD:]], axis=0)


def turned(ref):
    return jnp.concatenate([ref[HD : 3 * HD], ref[0:HD]], axis=0)


def token_grad_kernel(grad_ref, weight_ref, out_ref):
    for pair in range(RANKS // 2):
        rows = weight_ref[2 * pair : 2 * pair + 2].reshape(2 * HD, -1)
        both = dot_nt(grad_ref[...], rows)
        out_ref[2 * pair] = fold_rows(both[:, :HD]).astype(BF16)
        out_ref[2 * pair + 1] = fold_rows(both[:, HD:]).astype(BF16)


def project_kernel(
    place_ref, t0_ref, t1_ref, t2_ref, t3_ref, own_ref, other_ref,
    kv_ref, q_ref, swap_ref, far_ref, near_ref, far2_ref, near2_ref,
    kv32, kv32b,
):
    first_core = place_ref[2] == 0
    own, other = turned(own_ref), turned(other_ref)
    for chunk, (a_ref, b_ref) in enumerate(((t0_ref, t1_ref), (t2_ref, t3_ref))):
        rows = jnp.concatenate([a_ref[...], b_ref[...]], axis=0)
        proj = dot_nt(rows, own).astype(BF16).astype(F32)
        proj2 = dot_nt(rows, other).astype(BF16).astype(F32)
        for part in range(4):
            row = lax.rem(place_ref[0] + 8 - DISTANCE[chunk * 4 + part], 8)
            piece = proj[part * TOK : (part + 1) * TOK]
            kv32[row] = piece[:, :128]
            kv_ref[row] = piece[:, :128].astype(BF16)
            q_ref[row] = piece[:, 128:].astype(BF16)
            piece = proj2[part * TOK : (part + 1) * TOK]
            kv32b[row] = piece[:, :128]
            swap_ref[row] = piece.astype(BF16)
    west, east = pack_pair(kv32[...])
    far_ref[...] = jnp.where(first_core, west, east).astype(BF16)
    near_ref[...] = jnp.where(first_core, east, west).astype(BF16)
    west, east = pack_pair(kv32b[...])
    far2_ref[...] = jnp.where(first_core, west, east).astype(BF16)
    near2_ref[...] = jnp.where(first_core, east, west).astype(BF16)


def attend_kernel(
    place_ref, kv_ref, q_ref, swapped_ref, grad_ref, far_ref, near_ref, far2_ref, near2_ref,
    out_ref, dq_ref, dkv_ref, to_far_ref, to_near_ref,
    keys, queries, halo, dhalo,
):
    scale = HD ** (-0.5)
    yl = place_ref[1]
    first_core = place_ref[2] == 0
    far, near = far_ref[...].astype(F32), near_ref[...].astype(F32)
    side = unpack_pair(jnp.where(first_core, near, far), jnp.where(first_core, far, near))
    far, near = far2_ref[...].astype(F32), near2_ref[...].astype(F32)
    side2 = unpack_pair(jnp.where(first_core, near, far), jnp.where(first_core, far, near))
    for row in range(8):
        mine, theirs = 2 * row + yl, 2 * row + 1 - yl
        keys[mine] = kv_ref[row].astype(F32)
        queries[mine] = q_ref[row].astype(F32)
        both = swapped_ref[row].astype(F32)
        keys[theirs] = both[:, :128]
        queries[theirs] = both[:, 128:]
        halo[mine] = side[row // 4][row % 4]
        halo[theirs] = side2[row // 4][row % 4]
    zeros = jnp.zeros((2 * TOK, HD), F32)
    windows = RANKS // 2
    for w in range(windows):
        lo, hi = max(2 * w - 1, 0), min(2 * w + 3, RANKS)
        count = (hi - lo) * TOK
        query = queries[2 * w : 2 * w + 2].reshape(2 * TOK, HD) * scale
        outer = jnp.concatenate(
            [unfold_rows(grad_ref[2 * w + i].astype(F32)) for i in range(2)], axis=0
        )
        lhs = jnp.concatenate(
            [
                jnp.concatenate([query, zeros], axis=1),
                jnp.concatenate([zeros, outer], axis=1),
            ],
            axis=0,
        ).astype(BF16)
        pairs = jnp.concatenate(
            [keys[lo:hi].reshape(count, 128), halo[lo:hi].reshape(count, 128)], axis=0
        ).astype(BF16)
        both = dot_nt(lhs, pairs)
        score, prob_grad = both[: 2 * TOK], both[2 * TOK :]
        powers = jnp.exp(score - jnp.max(score, axis=-1, keepdims=True))
        probs = powers * (1.0 / jnp.sum(powers, axis=-1, keepdims=True))
        centre = jnp.sum(probs * prob_grad, axis=-1, keepdims=True)
        score_grad = (probs * (prob_grad - centre)).astype(BF16)
        stack = jnp.concatenate([score_grad, probs.astype(BF16)], axis=0)
        mixed = dot_nn(stack, pairs)
        dq_ref[2 * w : 2 * w + 2] = (mixed[: 2 * TOK, :HD] * scale).reshape(2, TOK, HD)
        for i in range(2):
            rows = mixed[(2 + i) * TOK : (3 + i) * TOK, HD:]
            out_ref[2 * w + i] = fold_rows(rows).astype(BF16)
        grads = dot_tn(stack, lhs)
        own = grads[:count].reshape(hi - lo, TOK, 128)
        side = grads[count:].reshape(hi - lo, TOK, 128)
        for i, rank in enumerate(range(lo, hi)):
            seen = w > 0 and rank <= 2 * w
            if seen:
                dkv_ref[rank] += own[i]
                dhalo[rank] += side[i]
            else:
                dkv_ref[rank] = own[i]
                dhalo[rank] = side[i]
    to_e, to_w = pack_pair(dhalo[...])
    to_far_ref[...] = jnp.where(first_core, to_w, to_e).astype(BF16)
    to_near_ref[...] = jnp.where(first_core, to_e, to_w).astype(BF16)


def combine_kernel(
    place_ref, dq_ref, dkv_ref, far_ref, near_ref, pg_ref, mine_ref, swap_ref, pg32
):
    yl = place_ref[1]
    first_core = place_ref[2] == 0
    far, near = far_ref[...].astype(F32), near_ref[...].astype(F32)
    first, second = unpack_pair(jnp.where(first_core, far, near), jnp.where(first_core, near, far))
    for half, add in ((0, first), (1, second)):
        span = slice(8 * half, 8 * half + 8)
        pg32[span, :, 0:128] = dkv_ref[span] + add
        pg32[span, :, 128:192] = dq_ref[span]
    pg_ref[...] = pg32[...].astype(BF16)
    for row in range(8):
        mine_ref[row] = pg32[2 * row + yl].astype(BF16)
        swap_ref[row] = pg32[2 * row + 1 - yl].astype(BF16)


def share_kernel(place_ref, mine_ref, got_ref, own_ref, other_ref, *out_refs):
    own, other = turned(own_ref), turned(other_ref)
    for chunk in range(2):
        reach = (6, 7, 1, 0) if chunk else (5, 4, 3, 2)
        picks = [lax.rem(place_ref[0] + r, 8) for r in reach]
        rows = jnp.concatenate([mine_ref[p].astype(F32) for p in picks], axis=0).astype(BF16)
        rows2 = jnp.concatenate([got_ref[p].astype(F32) for p in picks], axis=0).astype(BF16)
        part = (dot_nn(rows, own) + dot_nn(rows2, other)).astype(BF16)
        if chunk == 0:
            out_refs[0][...] = part[: 2 * TOK]
            out_refs[1][...] = part[2 * TOK :]
        else:
            for i in range(4):
                out_refs[2 + i][...] = part[i * TOK : (i + 1) * TOK]


def weight_grad_kernel(place_ref, pg_ref, *refs):
    total, piece_ref = None, refs[8]
    yl = place_ref[1]
    for chunk in range(4):
        parity = yl if chunk < 2 else 1 - yl
        near = DISTANCE[4 * (chunk % 2) : 4 * (chunk % 2) + 4]
        ranks = [2 * lax.rem(place_ref[0] + 8 - d, 8) + parity for d in near]
        rows = jnp.concatenate([pg_ref[r].astype(F32) for r in ranks], axis=0).astype(BF16)
        source = jnp.concatenate([refs[2 * chunk][...], refs[2 * chunk + 1][...]], axis=0)
        part = dot_tn(rows, source)
        total = part if total is None else total + part
    total = jnp.concatenate([total[128:192], total[0:128]], axis=0).astype(BF16)
    for g in range(4):
        for j in range(8):
            piece_ref[8 * g + j] = total[48 * g : 48 * g + 48, 128 * j : 128 * j + 128]


def mix_kernel(att_ref, weight_ref, out_ref):
    rows = [unfold_rows(att_ref[h].astype(F32)) for h in range(RANKS)]
    rows = jnp.concatenate(rows, axis=1).astype(BF16)
    out_ref[...] = dot_nn(rows, weight_ref[...]).astype(BF16)


def shift(value, axis, size, distance):
    return lax.ppermute(value, axis, [(i, (i + distance) % size) for i in range(size)])


def exchange(value, axis):
    return lax.all_to_all(value, axis, 0, 0, tiled=True)


def step(latents, out_grad, qkv_weight, out_weight):
    width = latents.shape[-1]
    z, yl, core = (lax.axis_index(a).astype(jnp.int32) for a in ("z", "yl", "core"))
    mine = latents.reshape(TOK, width)
    own = jnp.swapaxes(qkv_weight[0], 0, 1)
    other = shift(own, "yl", 2, 1)
    d7, d2, d1 = (shift(mine, "z", 8, d) for d in (7, 2, 1))
    pair0 = jnp.concatenate([mine, d7], axis=0)
    pair1 = jnp.concatenate([d1, d2], axis=0)
    pair2 = shift(pair0, "z", 8, -2)
    pair3 = shift(pair1, "z", 8, 2)
    tokens = (pair0, pair1, pair2, pair3)
    late0, late1 = shift(pair0, "yl", 2, 1), shift(pair1, "yl", 2, 1)
    late2, late3 = shift(pair2, "yl", 2, 1), shift(late1, "z", 8, 2)
    place = jnp.stack([z, yl, core])

    (token_grad,) = call(
        token_grad_kernel, [((RANKS, 40, 128), BF16)], n_in=2, flops=2 * TOK * width * width
    )(out_grad.reshape(TOK, width), out_weight)
    band_grad = exchange(token_grad, HEAD)

    kv, query, swap, far, near, far2, near2 = call(
        project_kernel,
        [((8, TOK, 128), BF16), ((8, TOK, HD), BF16), ((8, TOK, 3 * HD), BF16)]
        + [((4, TOK, 128), BF16)] * 4,
        scratch=[pltpu.VMEM((8, TOK, 128), F32)] * 2,
        smem=(0,),
        n_in=7,
        grant=12,
        flops=2 * 1152 * 192 * width,
    )(place, *tokens, own, other)
    far, near = send_far(far), shift(near, "core", 2, 1)
    far2, near2 = send_far(far2, 1), send_near(near2, 1)
    swapped = shift(swap, "yl", 2, 1)
    attended, dq, dkv, grad_far, grad_near = call(
        attend_kernel,
        [
            ((RANKS, 40, 128), BF16),
            ((RANKS, TOK, HD), F32),
            ((RANKS, TOK, 128), F32),
            ((8, TOK, 128), BF16),
            ((8, TOK, 128), BF16),
        ],
        scratch=[
            pltpu.VMEM((RANKS, TOK, 128), F32),
            pltpu.VMEM((RANKS, TOK, HD), F32),
            pltpu.VMEM((RANKS, TOK, 128), F32),
            pltpu.VMEM((RANKS, TOK, 128), F32),
        ],
        smem=(0,),
        n_in=9,
        flops=8 * 6 * 2 * 144 * 576 * 128,
    )(place, kv, query, swapped, band_grad, far, near, far2, near2)
    grad_far, grad_near = send_far(grad_far), shift(grad_near, "core", 2, 1)
    token_att = exchange(attended, HEAD)

    pg, pg_mine, pg_swap = call(
        combine_kernel,
        [((RANKS, TOK, 3 * HD), BF16), ((8, TOK, 3 * HD), BF16), ((8, TOK, 3 * HD), BF16)],
        scratch=[pltpu.VMEM((RANKS, TOK, 3 * HD), F32)],
        smem=(0,),
        n_in=5,
        flops=1 << 20,
    )(place, dq, dkv, grad_far, grad_near)
    pg_got = shift(pg_swap, "yl", 2, 1)
    (pieces,) = call(
        weight_grad_kernel,
        [((32, 48, 128), BF16)],
        smem=(0,),
        n_in=10,
        flops=2 * 1152 * 192 * width,
    )(place, pg, *tokens, late0, late1, late2, late3)
    pieces = exchange(pieces, LON)
    shares = call(
        share_kernel,
        [((2 * TOK, width), BF16)] * 2 + [((TOK, width), BF16)] * 4,
        smem=(0,),
        n_in=5,
        flops=2 * 576 * 384 * width,
    )(place, pg_mine, pg_got, own, other)
    down, up, s6, s7, s1, s0 = shares
    down, up = shift(down, "z", 8, -2), shift(up, "z", 8, 2)
    s7 = (s7.astype(F32) + down[:TOK].astype(F32)).astype(BF16)
    s6 = (s6.astype(F32) + down[TOK:].astype(F32)).astype(BF16)
    s1 = (s1.astype(F32) + up[:TOK].astype(F32)).astype(BF16)
    shares = [shift(s6, "z", 8, -2), shift(s7, "z", 8, -1)]
    shares = [s0, up[TOK:], shift(s1, "z", 8, 1)] + shares
    summed = jnp.sum(pieces.astype(F32), axis=0).astype(BF16)
    copies = exchange(jnp.broadcast_to(summed[None], (32, 48, 128)), LON)
    (mixed,) = call(
        mix_kernel, [((TOK, width), BF16)], n_in=2, flops=2 * TOK * width * width, grant=12
    )(
        token_att, out_weight.reshape(width, width)
    )
    grad = copies.reshape(4, 8, 48, 128).transpose(0, 2, 1, 3).reshape(3 * HD, width).astype(F32)
    grad, *shares = lax.optimization_barrier((grad, *shares))
    latent_grad = sum(s.astype(F32) for s in shares).astype(BF16)
    qkv_grad = jnp.swapaxes(grad, 0, 1)[None]
    return mixed.reshape(latents.shape), latent_grad.reshape(latents.shape), qkv_grad


def send_far(value, turn=0):
    routes = [
        (2 * i + j, 2 * ((i + (1 if i % 2 else -1)) % 32) + (j ^ turn))
        for i in range(32)
        for j in range(2)
    ]
    return lax.ppermute(value, LON + ("yl",), routes)


def send_near(value, turn=0):
    routes = [(2 * i + j, 2 * (i ^ 1) + (j ^ turn)) for i in range(32) for j in range(2)]
    return lax.ppermute(value, LON + ("yl",), routes)


def solution(mesh):
    split = Mesh(mesh.devices.reshape(4, 4, 2, 8, 2), LON + HEAD)
    rows = P(None, HEAD, LON, None)
    return jax.shard_map(
        step,
        mesh=split,
        in_specs=(rows, rows, P(HEAD, None, None), P()),
        out_specs=(rows, rows, P(HEAD, None, None)),
        check_vma=False,
    )
```
